32 devices in a mesh: dp: 8 (over y, x, core), seq: 4 (over z).
Axes of the slice: x: 2, y: 2, z: 4, core: 2. Of those that a mesh axis runs over, the one named last changes fastest.
Arguments:
- tokens: int32 [8, 1024], P('dp', 'seq'), may hold values from 0 to 3
- embedding: float32 [4, 384], replicated, may hold values from -6 to 6
- gain_in: float32 [384], replicated, may hold values from 0.5 to 1.5
- conv_taps: float32 [384, 4], replicated, may hold values from -3 to 3
- long_filter: float32 [384, 1024], P('seq'), may hold values from -6 to 6
- gain_mid: float32 [384], replicated, may hold values from 0.5 to 1.5
- mlp_weights: bfloat16 [2304, 384], replicated, may hold values from -0.3125 to 0.3125
- cotangent: bfloat16 [8, 768, 1024], P('dp', None, 'seq'), may hold values from -6 to 6
Outputs:
- layer_out: bfloat16 [8, 768, 1024], P('dp', None, 'seq')
- grad_embedding: float32 [4, 384], replicated
- grad_gain_in: float32 [384], replicated
- grad_conv: float32 [384, 4], replicated
- grad_filter: float32 [384, 1024], P('seq')
- grad_gain_mid: float32 [384], replicated
- grad_mlp: float32 [2304, 384], P('dp', 'seq')
The draws below stay inside these ranges and needn't reach their ends.
All inputs are finite; a program needn't handle non-finite values.
Results may differ from the reference program's by a relative error of at most 0.03.
Values may be sent and summed in bfloat16 or wider, within the bound.
A program may use at most 64 MiB of HBM per device.

```python
from functools import partial
import jax
import jax.numpy as jnp
from jax import lax

D = 384
FF = 768
GROUP = 1024
KW = 4
LEN = 1024
BATCH = 8


def plant(values, key, least, top_value):
    extent = values.shape
    spot = [jax.random.randint(jax.random.fold_in(key, axis), (), 0, extent[axis]) for axis in range(len(extent))]
    values = values.at[tuple(spot)].set(least)
    longest = extent.index(max(extent))
    spot[longest] = (spot[longest] + 1) % extent[longest]
    return values.at[tuple(spot)].set(top_value)


def steps_of(own_key, shape, shards, least, high):
    loudness, own = 1.0, jax.random.fold_in(own_key, 6)
    for axis_at, shards_of in shards:
        draws = jnp.exp(jax.random.uniform(jax.random.fold_in(own, axis_at), (shards_of,), jnp.float32, least / len(shards), high / len(shards)))
        loudness = loudness * jnp.repeat(draws, shape[axis_at] // shards_of).reshape([-1 if axis == axis_at else 1 for axis in range(len(shape))])
    return loudness


def bell_draw(stream_key, shape, spread, reach, cuts=(), kind=jnp.bfloat16):
    values = spread * jax.random.normal(stream_key, shape, jnp.float32)
    if cuts:
        values = values * steps_of(stream_key, shape, cuts, -0.22, 0.18)
    return jnp.clip(values, -reach, reach).astype(kind)


def setup_inputs(seed: int = 0) -> dict:
    streams_of = jax.random.split(jax.random.key(seed), 9)
    tokens = plant(jax.random.randint(streams_of[0], (BATCH, LEN), 0, 4), jax.random.fold_in(streams_of[0], 1), 0, 3).astype(jnp.int32)
    embedding = bell_draw(streams_of[1], (4, D), 1.0, 6.0, (), jnp.float32)
    gain_in = jnp.clip(1.0 + 0.1 * jax.random.normal(streams_of[2], (D,), jnp.float32), 0.5, 1.5)
    conv_taps = bell_draw(streams_of[3], (D, KW), KW ** -0.5, 3.0, (), jnp.float32)
    long_filter = bell_draw(streams_of[4], (D, GROUP), 1.0, 6.0, ((0, 4),), jnp.float32)
    gain_mid = jnp.clip(1.0 + 0.1 * jax.random.normal(streams_of[5], (D,), jnp.float32), 0.5, 1.5)
    mlp_weights = bell_draw(streams_of[6], (3 * FF, D), D ** -0.5, 0.3125)
    cotangent = bell_draw(streams_of[7], (BATCH, 2 * D, LEN), 1.0, 6.0, ((0, 8), (2, 4)))
    return dict(tokens=tokens, embedding=embedding, gain_in=gain_in, conv_taps=conv_taps, long_filter=long_filter, gain_mid=gain_mid, mlp_weights=mlp_weights, cotangent=cotangent)


def dct_table(length):
    freq = jnp.arange(length, dtype=jnp.int32)[:, None]
    place = jnp.arange(length, dtype=jnp.int32)[None, :]
    phase = (2 * place + 1) * freq % (4 * length)
    weight = jnp.where(freq == 0, jnp.sqrt(1.0 / length), jnp.sqrt(2.0 / length))
    angle = jnp.pi * phase.astype(jnp.float32) / (2 * length)
    return (weight * jnp.cos(angle)).astype(jnp.bfloat16)

def rms_gain(values, gain):
    scale = lax.rsqrt(lax.optimization_barrier(jnp.mean(values * values, axis=-2, keepdims=True)) + 1e-06)
    return (values * scale * gain[:, None]).astype(jnp.bfloat16)

def lookup_norm(embedding, gain_in, onehot):
    residual = jnp.einsum('kd,sbkl->sbdl', embedding, onehot, precision=lax.Precision.HIGHEST)
    return (residual, rms_gain(residual, gain_in))

def conv_before(padded, conv_taps):
    rim_width = conv_taps.shape[1] - 1
    length = padded.shape[-1] - rim_width
    summed = conv_taps[:, 0][:, None] * padded[..., rim_width:rim_width + length]
    for tap_index in range(1, rim_width + 1):
        start = rim_width - tap_index
        summed = summed + conv_taps[:, tap_index][:, None] * padded[..., start:start + length]
    return summed.astype(jnp.bfloat16)

def group_filter(mixed, long_filter, dct_rows):
    strands, batch, channels, length = mixed.shape
    block_len = dct_rows.shape[0]
    blocks = mixed.astype(jnp.float32).reshape(strands, batch, channels, length // block_len, block_len)
    table_f = dct_rows.astype(jnp.float32)
    spectrum = jnp.einsum('sbdni,ki->sbdnk', blocks, table_f, precision=lax.Precision.HIGHEST).astype(jnp.bfloat16)
    scaled = (long_filter[None, None, :, None, :] * spectrum.astype(jnp.float32)).astype(jnp.bfloat16)
    restored = jnp.einsum('sbdnk,ki->sbdni', scaled.astype(jnp.float32), table_f, precision=lax.Precision.HIGHEST)
    return restored.astype(jnp.bfloat16).reshape(strands, batch, channels, length)

def mid_norm(residual, filtered, gain_mid):
    level = residual + filtered.astype(jnp.float32)
    return (level, rms_gain(level, gain_mid))

def feed_forward(level, normed_mid, weights):
    projected = jnp.einsum('fd,sbdl->sbfl', weights[:2 * FF], normed_mid.astype(jnp.float32), precision=lax.Precision.HIGHEST).astype(jnp.bfloat16)
    both_parts = projected.astype(jnp.float32)
    gate_in = both_parts[:, :, :FF]
    up_value = both_parts[:, :, FF:]
    activated = (jax.nn.silu(gate_in) * up_value).astype(jnp.bfloat16)
    down = jnp.einsum('fd,sbfl->sbdl', weights[2 * FF:], activated.astype(jnp.float32), precision=lax.Precision.HIGHEST)
    return (level + down).astype(jnp.bfloat16)

def strand_layer(base_ids, dct_rows, embedding, gain_in, conv_taps, long_filter, gain_mid, weights):
    strands = jnp.stack([base_ids, 3 - jnp.flip(base_ids, 0)])[:, None, :]
    onehot = (strands[:, :, None, :] == jnp.arange(4, dtype=jnp.int32)[None, None, :, None]).astype(jnp.float32)
    residual, normed = lookup_norm(embedding, gain_in, onehot)
    padded = jnp.pad(normed.astype(jnp.float32), ((0, 0), (0, 0), (0, 0), (KW - 1, 0)))
    mixed = conv_before(padded, conv_taps)
    filtered = group_filter(mixed, long_filter, dct_rows)
    level, normed_mid = mid_norm(residual, filtered, gain_mid)
    result = feed_forward(level, normed_mid, weights)
    return jnp.concatenate([result[0, 0], jnp.flip(result[1, 0], (0, 1))], 0)

def reference(tokens, embedding, gain_in, conv_taps, long_filter, gain_mid, mlp_weights, cotangent):
    dct_rows = dct_table(GROUP)
    params = (embedding, gain_in, conv_taps, long_filter, gain_mid, mlp_weights.astype(jnp.float32))

    def one_sequence(running, sliced):
        base_ids, seq_cot = sliced
        layer_part, pullback = jax.vjp(partial(strand_layer, base_ids, dct_rows), *params)
        gradients = pullback(seq_cot)
        return (tuple((summed_grad + fresh_grad for summed_grad, fresh_grad in zip(running, gradients))), layer_part)
    zeros = tuple((jnp.zeros(param.shape, jnp.float32) for param in params))
    totals, layer_out = lax.scan(one_sequence, zeros, (tokens, cotangent))
    return (layer_out, totals[0], totals[1], totals[2], totals[3], totals[4], totals[5])
```

```python
import jax
import jax.numpy as jnp
import numpy as np
from jax import lax
from jax.experimental import pallas as pl
from jax.experimental.pallas import tpu as pltpu
from jax.sharding import PartitionSpec as P

F32 = jnp.float32
BF16 = jnp.bfloat16


def dct_table(length):
    freq = np.arange(length)[:, None]
    place = np.arange(length)[None, :]
    phase = (2 * place + 1) * freq % (4 * length)
    weight = np.where(freq == 0, np.sqrt(1.0 / length), np.sqrt(2.0 / length))
    return (weight * np.cos(np.pi * phase / (2 * length))).astype(np.float32).astype(BF16)


def dot(a, b, dims):
    return lax.dot_general(a, b, (dims, ((), ())), preferred_element_type=F32)


MESH = pl.DeviceIdType.MESH
TILE = 16


def flip(index, mask):
    bit = 1
    while bit <= mask:
        if mask & bit:
            index = index + bit * (1 - 2 * lax.rem(index // bit, 2))
        bit *= 2
    return index


def chunk_rows(part):
    units = part // TILE
    sizes = [TILE * ((units + 3 - i) // 4) for i in range(4)]
    sizes[3] += part - sum(sizes)
    return sizes


def stage_masks(order, stage, count):
    sent = [
        r
        for r in range(count)
        if (r >> order[stage]) & 1 and not any((r >> o) & 1 for o in order[:stage])
    ]
    return sorted(sent, key=lambda r: [-((r >> o) & 1) for o in order[stage + 1 :]])


class Sems:
    def __init__(self, send, recv):
        self.send, self.recv, self.used, self.started = send, recv, 0, []

    def take(self, count=1):
        first = self.used
        self.used += count
        return first

    def copy(self, index, src, dst, peer):
        return pltpu.make_async_remote_copy(
            src_ref=src,
            dst_ref=dst,
            send_sem=self.send.at[index],
            recv_sem=self.recv.at[index],
            device_id=peer,
            device_id_type=MESH,
        )

    def start(self, index, src, dst, peer):
        copy = self.copy(index, src, dst, peer)
        copy.start()
        self.started.append(copy)

    def arrived(self, index, dst, peer):
        self.copy(index, dst, dst, peer).wait_recv()

    def drain(self):
        for copy in self.started:
            copy.wait_send()


class Stream:
    def __init__(self, sems, order, place, recs):
        self.sems, self.order, self.place, self.recs = sems, order, place, recs
        self.count = 2 ** len(order)
        self.base = [sems.take(len(stage_masks(order, s, self.count))) for s in range(len(order))]

    def send_one(self, stage, mask, dp, sq):
        slot = stage_masks(self.order, stage, self.count).index(mask)
        peer = (flip(dp, 2 << self.order[stage]), sq)
        self.sems.start(
            self.base[stage] + slot, self.place(flip(dp // 2, mask)), self.recs[stage].at[slot], peer
        )

    def send_first(self, dp, sq, which):
        masks = stage_masks(self.order, 0, self.count)
        self.send_one(0, masks[which], dp, sq)

    def take_in(self, stage, dp, sq):
        for slot, mask in enumerate(stage_masks(self.order, stage, self.count)):
            kept = mask ^ (1 << self.order[stage])
            self.sems.arrived(self.base[stage] + slot, self.recs[stage].at[slot], (dp, sq))
            ref = self.place(flip(dp // 2, kept))
            ref[...] = (ref[...].astype(F32) + self.recs[stage][slot].astype(F32)).astype(BF16)
            if stage + 1 < len(self.order) and (kept >> self.order[stage + 1]) & 1:
                self.send_one(stage + 1, kept, dp, sq)


def sem_count(n_dp, n_seq, lanes_in):
    far, pairs = n_seq - 1, n_dp // 2
    bits = n_dp.bit_length() - 1
    return 2 * far + far * lanes_in + 4 * pairs + 2 + 6 * (pairs - 1) + bits + far + 6 * far + n_dp


def mega_kernel(
    n_dp, n_seq, lanes_in,
    ids, emb, gin, gmid, taps_in, shard, table_h, mlp_h, cot_h,
    out, mlp_out, filt_out, small_out,
    table, mlp, cot, gath, all_ids, full, spec_ref, level_ref, normed_ref, d_normed_ref, down_ref, d_act_ref,
    g0, g1, g2, g3, r0, r1, r2, r3, m0, m1, m2, m3,
    gf, rf, mf, z0, z1, z2, z3, y0, y1, y2, y3, yf, mine,
    sm, s_rec, s_acc, zs_rec,
    *rest,
):
    bits = n_dp.bit_length() - 1
    pairs = n_dp // 2
    stage_bufs = list(rest[: 6 * (bits - 1)])
    load_sem, send, recv = rest[6 * (bits - 1) :]
    sems = Sems(send, recv)
    grads, recs0, sums = (g0, g1, g2, g3), (r0, r1, r2, r3), (m0, m1, m2, m3)
    z_out, z_in = (z0, z1, z2, z3), (y0, y1, y2, y3)
    own_rows, block_len = shard.shape
    channels = own_rows * n_seq
    local_len = ids.shape[1]
    hidden = mlp.shape[0] // 3
    n_taps = taps_in.shape[0]
    half = 4 * n_taps
    part = mlp.shape[0] // n_dp
    sizes = chunk_rows(part)
    dp, sq = lax.axis_index("dp"), lax.axis_index("seq")
    core = lax.rem(dp, 2)
    me_q = dp // 2
    mate = (flip(dp, 1), sq)
    here = (dp, sq)
    wide = block_len // lanes_in
    lane_at = lax.rem(dp, lanes_in)

    loads = [
        pltpu.make_async_copy(table_h, table, load_sem.at[0]),
        pltpu.make_async_copy(cot_h, cot, load_sem.at[1]),
        pltpu.make_async_copy(mlp_h, mlp, load_sem.at[2]),
    ]
    for load in loads:
        load.start()
    barrier = pltpu.get_barrier_semaphore()
    for mask in range(1, n_dp):
        pl.semaphore_signal(barrier, inc=1, device_id=(flip(dp, mask), sq), device_id_type=MESH)
    for mask in range(1, n_seq):
        pl.semaphore_signal(barrier, inc=1, device_id=(dp, flip(sq, mask)), device_id_type=MESH)
    for p in range(lanes_in):
        gath[p, sq] = shard[:, p * wide : (p + 1) * wide].astype(BF16)
    all_ids[sq] = ids[...]
    pl.semaphore_wait(barrier, n_dp + n_seq - 2)

    id_base = sems.take(n_seq - 1)
    z_base = sems.take(n_seq - 1)
    for k in range(1, n_seq):
        to = (dp, flip(sq, k))
        sems.start(id_base + k - 1, ids, all_ids.at[sq], to)
        sems.start(z_base + k - 1, gath.at[lane_at, sq], gath.at[lane_at, sq], to)

    pad = 128 - 6 - n_taps
    rows_all = jnp.concatenate(
        [
            emb[...],
            gin[...].reshape(1, channels),
            gmid[...].reshape(1, channels),
            taps_in[...],
            jnp.zeros((pad, channels), F32),
        ],
        0,
    )
    packed = rows_all.T
    emb_cols, gain_in, gain_mid = packed[:, :4], packed[:, 4:5], packed[:, 5:6]
    taps = packed[:, 6 : 6 + n_taps]
    base_scale = lax.rsqrt(jnp.mean(emb_cols * emb_cols, axis=0, keepdims=True) + 1e-6)
    base_norm = (emb_cols * base_scale * gain_in).astype(BF16).astype(F32)
    lane = lax.broadcasted_iota(jnp.int32, (channels, half), 1)
    tap_part = jnp.zeros((channels, half), F32)
    base_part = jnp.zeros((channels, half), F32)
    for k in range(n_taps):
        tap_part = jnp.where(lane // 4 == k, taps[:, k : k + 1], tap_part)
    for a in range(4):
        base_part = jnp.where(lane % 4 == a, base_norm[:, a : a + 1], base_part)
    kmer = (tap_part * base_part).astype(BF16)
    turn = jnp.where(
        lax.broadcasted_iota(jnp.int32, (channels, channels), 0)
        + lax.broadcasted_iota(jnp.int32, (channels, channels), 1)
        == channels - 1,
        1.0,
        0.0,
    ).astype(BF16)
    loads[1].wait()
    turned = dot(turn, cot[channels:, :], ((1,), (0,))).astype(BF16)
    back = jnp.concatenate([cot[:channels, :], turned], 1)

    masks = [*range(2, lanes_in, 2)]
    near = [0] + masks if lanes_in > 1 else []
    far_base = sems.take((n_seq - 1) * len(masks))
    mate_base = sems.take((n_seq - 1) * len(near))

    def to_mate(k, n):
        piece = gath.at[flip(lane_at, near[n]), flip(sq, k)]
        sems.start(mate_base + (k - 1) * len(near) + n, piece, piece, mate)

    for k in range(1, n_seq):
        piece = gath.at[lane_at, flip(sq, k)]
        sems.arrived(z_base + k - 1, piece, here)
        for n, mask in enumerate(masks):
            sems.start(far_base + (k - 1) * len(masks) + n, piece, piece, (flip(dp, mask), sq))
        if near:
            to_mate(k, 0)
    for k in range(1, n_seq):
        sems.arrived(id_base + k - 1, all_ids.at[flip(sq, k)], here)

    per_block = block_len // local_len
    first = sq // per_block * per_block
    last = first + per_block - 1
    offset = pl.multiple_of((sq - first) * local_len, local_len)
    edge = 128
    before = jnp.where(first > 0, all_ids[jnp.maximum(first - 1, 0)][:, local_len - edge :], 4)
    after = jnp.where(last < n_seq - 1, all_ids[jnp.minimum(last + 1, n_seq - 1)][:, :edge], 4)
    row = jnp.concatenate([before] + [all_ids[first + j] for j in range(per_block)] + [after], 1)
    width = block_len + 2 * edge
    spread = jnp.broadcast_to(row, (8, width))
    sub = lax.broadcasted_iota(jnp.int32, (8, block_len), 0)
    tiles = []
    for s in range(2):
        for k in range(0, n_taps, 2):
            shifts = [(k + i) if s == 0 else (width - k - i) % width for i in range(2)]
            moved = [(pltpu.roll(spread, sh, 1) if sh else spread)[:, edge : edge + block_len] for sh in shifts]
            picked = jnp.where(sub < 4, moved[0], moved[1])
            want = sub % 4 if s == 0 else 3 - sub % 4
            tiles.append(jnp.where(picked == want, 1.0, 0.0))
    hot = jnp.concatenate(tiles, 0).astype(BF16)
    loads[0].wait()
    hot_spec = dot(hot, table[...], ((1,), (0,))).astype(BF16)
    for s in range(2):
        spec_ref[s] = dot(kmer, hot_spec[s * half : (s + 1) * half], ((1,), (0,))).astype(BF16)
    loads[2].wait()
    d_act_ref[...] = dot(mlp[2 * hidden :, :], back, ((1,), (0,)))

    for k in range(1, n_seq):
        for n, mask in enumerate(masks):
            piece = gath.at[flip(lane_at, mask), flip(sq, k)]
            sems.arrived(far_base + (k - 1) * len(masks) + n, piece, here)
            to_mate(k, n + 1)
    for k in range(1, n_seq):
        for n in range(len(near)):
            piece = gath.at[flip(lane_at, near[n] + 1), flip(sq, k)]
            sems.arrived(mate_base + (k - 1) * len(near) + n, piece, here)

    for p in range(lanes_in):
        full[:, p * wide : (p + 1) * wide] = gath[p].astype(F32).reshape(channels, wide)
    own = ids[...]
    q_own = table[pl.ds(offset, local_len), :]
    for s in range(2):
        scaled = (full[...] * spec_ref[s].astype(F32)).astype(BF16)
        mine_ids = own if s == 0 else 3 - own
        level = dot(scaled, q_own, ((1,), (1,)))
        residual = jnp.zeros((channels, local_len), F32)
        for a in range(4):
            residual = jnp.where(mine_ids == a, emb_cols[:, a : a + 1], residual)
        level_ref[:, s * local_len : (s + 1) * local_len] = level + residual
    level = level_ref[...]
    mid_scale = lax.rsqrt(jnp.mean(level * level, axis=0, keepdims=True) + 1e-6)
    normed_ref[...] = (level * mid_scale * gain_mid).astype(BF16)
    normed = normed_ref[...]

    edges = []
    for i in range(n_dp):
        at = i * part
        for c in range(4):
            edges.append((at, at + sizes[c], i, c))
            at += sizes[c]
    filled = {(i, c): 0 for i in range(n_dp) for c in range(4)}
    core_base = sems.take(4 * pairs)
    gone = set()

    def put(start, value):
        for lo, hi, i, c in edges:
            a, b = max(lo, start), min(hi, start + value.shape[0])
            if a < b:
                grads[c][i % 2, i // 2, a - lo : b - lo, :] = value[a - start : b - start, :]
                filled[i, c] += b - a

    def swap_done():
        for c in range(4):
            for q in range(pairs):
                if (c, q) not in gone and filled[2 * q, c] == sizes[c] and filled[2 * q + 1, c] == sizes[c]:
                    gone.add((c, q))
                    sems.start(core_base + c * pairs + q, grads[c].at[1 - core, q], recs0[c].at[q], mate)

    tile = 256 if hidden % 256 == 0 else hidden
    for t in range(hidden // tile):
        a0, u0, w0 = t * tile, hidden + t * tile, 2 * hidden + t * tile
        w_gate, w_up, w_down = mlp[a0 : a0 + tile, :], mlp[u0 : u0 + tile, :], mlp[w0 : w0 + tile, :]
        gate = dot(w_gate, normed, ((1,), (0,)))
        up = dot(w_up, normed, ((1,), (0,)))
        d_act = d_act_ref[a0 : a0 + tile, :]
        sig = jax.nn.sigmoid(gate)
        silu = gate * sig
        act = (silu * up).astype(BF16)
        d_gate = (d_act * up * (sig + silu * (1.0 - sig))).astype(BF16)
        d_up = (d_act * silu).astype(BF16)
        for start, left, right in ((a0, d_gate, normed), (u0, d_up, normed), (w0, act, back)):
            put(start, dot(left, right, ((1,), (1,))).astype(BF16))
        swap_done()
        down = dot(w_down, act, ((0,), (0,)))
        down_ref[...] = down if t == 0 else down_ref[...] + down
        d_part = dot(w_gate, d_gate, ((0,), (0,))) + dot(w_up, d_up, ((0,), (0,)))
        d_normed_ref[...] = d_part if t == 0 else d_normed_ref[...] + d_part

    order_a = [*range(bits - 1)]
    order_b = [*range(1, bits - 1)] + [0] if bits > 1 else []
    streams = []
    for c in range(4):
        recs = [stage_bufs[c * (bits - 1) + s] for s in range(bits - 1)]
        streams.append(Stream(sems, order_b if c % 2 else order_a, lambda q, c=c: sums[c].at[q], recs))
    split = n_seq // 2
    for c in range(2):
        recs = [stage_bufs[(4 + c) * (bits - 1) + s] for s in range(bits - 1)]
        lo, hi = (0, split) if c == 0 else (split, n_seq)
        streams.append(
            Stream(sems, order_b if c % 2 else order_a, lambda q, lo=lo, hi=hi: mf.at[q, pl.ds(lo, hi - lo)], recs)
        )
    n_first = len(stage_masks(order_a, 0, pairs)) if bits > 1 else 0

    def open_pair(lead):
        for c in (lead, lead + 1):
            for q in range(pairs):
                sems.arrived(core_base + c * pairs + q, recs0[c].at[q], here)
                sums[c][q] = (grads[c][core, q].astype(F32) + recs0[c][q].astype(F32)).astype(BF16)
        for which in range(n_first):
            for c in (lead, lead + 1):
                streams[c].send_first(dp, sq, which)

    def middle(lead):
        for stage in range(bits - 1):
            for c in (lead, lead + 1):
                streams[c].take_in(stage, dp, sq)

    cols = channels // n_seq
    zm_base = sems.take(4 * (n_seq - 1))

    def across(c):
        total = sums[c][me_q]
        for j in range(n_seq):
            z_out[c][j] = total[:, j * cols : (j + 1) * cols]
        for k in range(1, n_seq):
            sems.start(
                zm_base + c * (n_seq - 1) + k - 1, z_out[c].at[flip(sq, k)], z_in[c].at[k - 1], (dp, flip(sq, k))
            )

    open_pair(0)

    mid_level = level_ref[...]
    combined = (mid_level + down_ref[...]).astype(BF16)
    out[:channels, :] = combined[:, :local_len]
    out[channels:, :] = dot(turn, combined[:, local_len:], ((1,), (0,))).astype(BF16)
    unit = mid_level * mid_scale
    d_normed = d_normed_ref[...]
    mid_grad = d_normed * unit
    d_unit = d_normed * gain_mid
    d_level = back.astype(F32) + mid_scale * (d_unit - unit * jnp.mean(d_unit * unit, axis=0, keepdims=True))
    d_bf = d_level.astype(BF16)
    d_low = (d_level - d_bf.astype(F32)).astype(BF16)
    both = jnp.concatenate([own, 3 - own], 1)
    sub8 = lax.broadcasted_iota(jnp.int32, (8, 2 * local_len), 0)
    own_hot = jnp.where(sub8 == both, 1.0, 0.0).astype(BF16)
    ones = jnp.ones((8, 2 * local_len), BF16)
    m_bf = mid_grad.astype(BF16)
    m_low = (mid_grad - m_bf.astype(F32)).astype(BF16)
    base_part_sum = dot(own_hot, d_bf, ((1,), (1,))) + dot(own_hot, d_low, ((1,), (1,)))
    mid_part_sum = dot(ones, m_bf, ((1,), (1,))) + dot(ones, m_low, ((1,), (1,)))

    open_pair(2)

    grad_filter = jnp.zeros((channels, block_len), F32)
    kmer_sum = jnp.zeros((half, channels), F32)
    for s in range(2):
        d_scaled = dot(d_bf[:, s * local_len : (s + 1) * local_len], q_own, ((1,), (0,)))
        grad_filter = grad_filter + d_scaled * spec_ref[s].astype(F32)
        d_spec = (full[...] * d_scaled).astype(BF16)
        kmer_sum = kmer_sum + dot(hot_spec[s * half : (s + 1) * half], d_spec, ((1,), (1,)))
    grad_filter = grad_filter.astype(BF16)
    groups = n_dp // lanes_in
    piece_rows = own_rows // groups
    for i in range(n_dp):
        block = grad_filter[:, i % lanes_in * wide : (i % lanes_in + 1) * wide]
        for j in range(n_seq):
            top = j * own_rows + i // lanes_in * piece_rows
            gf[i % 2, i // 2, j] = block[top : top + piece_rows, :]
    rows_half = sm.shape[1]
    joined = jnp.concatenate([kmer_sum, base_part_sum, mid_part_sum], 0)
    sm[0] = joined[:rows_half]
    sm[1] = joined[rows_half:]
    f_base, s_base = sems.take(), sems.take(bits)
    sems.start(f_base, gf.at[1 - core], rf, mate)
    sems.start(s_base, sm.at[1 - core], s_rec.at[0], mate)

    middle(0)
    across(0)
    across(1)

    sems.arrived(f_base, rf, here)
    for q in range(pairs):
        mf[q] = (gf[core, q].astype(F32) + rf[q].astype(F32)).astype(BF16)
    for which in range(n_first):
        for c in (4, 5):
            streams[c].send_first(dp, sq, which)
    for b in range(bits):
        sems.arrived(s_base + b, s_rec.at[b], here)
        s_acc[b] = (sm[core] if b == 0 else s_acc[b - 1]) + s_rec[b]
        if b + 1 < bits:
            sems.start(s_base + b + 1, s_acc.at[b], s_rec.at[b + 1], (flip(dp, 2 << b), sq))
    zs_base = sems.take(n_seq - 1)
    zs_rec[sq] = s_acc[bits - 1]
    for k in range(1, n_seq):
        sems.start(zs_base + k - 1, s_acc.at[bits - 1], zs_rec.at[sq], (dp, flip(sq, k)))

    middle(4)
    zf_base = sems.take(n_seq - 1)
    for k in range(1, n_seq):
        sems.start(zf_base + k - 1, mf.at[me_q, flip(sq, k)], yf.at[k - 1], (dp, flip(sq, k)))
    middle(2)
    across(2)
    across(3)

    for k in range(1, n_seq):
        sems.arrived(zs_base + k - 1, zs_rec.at[flip(sq, k)], here)
    total = zs_rec[0]
    for j in range(1, n_seq):
        total = total + zs_rec[j]
    small_out[core] = total
    back_base = sems.take()
    sems.start(back_base, small_out.at[core], small_out.at[core], mate)

    total = mf[me_q, sq].astype(F32)
    for k in range(1, n_seq):
        sems.arrived(zf_base + k - 1, yf.at[k - 1], here)
        total = total + yf[k - 1].astype(F32)
    filt_out[dp] = total.astype(BF16)
    ring_base = sems.take(n_dp - 1)
    for mask in range(1, n_dp):
        sems.start(ring_base + mask - 1, filt_out.at[dp], filt_out.at[dp], (flip(dp, mask), sq))
    at = 0
    for c in range(4):
        total = z_out[c][sq].astype(F32)
        for k in range(1, n_seq):
            sems.arrived(zm_base + c * (n_seq - 1) + k - 1, z_in[c].at[k - 1], here)
            total = total + z_in[c][k - 1].astype(F32)
        mlp_out[at : at + sizes[c], :] = total
        at += sizes[c]
    sems.arrived(back_base, small_out.at[1 - core], here)
    for mask in range(1, n_dp):
        sems.arrived(ring_base + mask - 1, filt_out.at[flip(dp, mask)], here)
    sems.drain()


def finish_kernel(
    n_taps, layer, mlp_sum, filt, small, embedding, gain_in, taps,
    layer_out, grad_emb, grad_gain, grad_conv, filt_out, grad_mid, mlp_out,
):
    layer_out[...] = layer[...]
    mlp_out[...] = mlp_sum[...]
    n_dp, rows, wide = filt.shape
    lanes_in = filt_out.shape[1] // wide
    for i in range(n_dp):
        top, left = i // lanes_in * rows, i % lanes_in * wide
        filt_out[top : top + rows, left : left + wide] = filt[i].astype(F32)
    channels = embedding.shape[1]
    sums = jnp.concatenate([small[0], small[1]], 0)
    emb = embedding[...]
    gain = gain_in[...].reshape(1, channels)
    base_scale = lax.rsqrt(jnp.mean(emb * emb, axis=1, keepdims=True) + 1e-6)
    unit = emb * base_scale
    base_norm = (unit * gain).astype(BF16).astype(F32)
    d_norm = jnp.zeros(emb.shape, F32)
    for k in range(n_taps):
        part = sums[4 * k : 4 * k + 4, :]
        d_norm = d_norm + part * taps[k : k + 1, :]
        grad_conv[k : k + 1, :] = jnp.sum(part * base_norm, axis=0, keepdims=True)
    grad_gain[...] = jnp.sum(d_norm * unit, axis=0)
    d_unit = d_norm * gain
    base_sum = sums[4 * n_taps : 4 * n_taps + 4, :]
    grad_emb[...] = base_sum + base_scale * (d_unit - unit * jnp.mean(d_unit * unit, axis=1, keepdims=True))
    grad_mid[...] = sums[4 * n_taps + 8 : 4 * n_taps + 9, :].reshape(channels)


def on_device(tokens, embedding, gain_in, conv_taps, long_filter, gain_mid, mlp_weights, cotangent):
    n_dp, n_seq = lax.axis_size("dp"), lax.axis_size("seq")
    own_rows, block_len = long_filter.shape
    channels = own_rows * n_seq
    local_len = tokens.shape[1]
    lanes_in = n_dp
    while block_len % (lanes_in * 128):
        lanes_in //= 2
    wide = block_len // lanes_in
    table = jnp.asarray(dct_table(block_len).T)
    taps = conv_taps.T
    n_taps = taps.shape[0]
    pairs, bits = n_dp // 2, n_dp.bit_length() - 1
    part = mlp_weights.shape[0] // n_dp
    sizes = chunk_rows(part)
    cols = channels // n_seq
    piece = (own_rows // (n_dp // lanes_in), wide)
    rows_half = (4 * n_taps + 16) // 2
    orders = [[*range(bits - 1)], [*range(1, bits - 1)] + [0] if bits > 1 else []]
    two = 2 * local_len

    def v(shape, dtype=BF16):
        return pltpu.VMEM(shape, dtype)

    stage_bufs = []
    for c in range(6):
        order = orders[c % 2]
        split = n_seq // 2
        tail = (sizes[c], channels) if c < 4 else ((split if c == 4 else n_seq - split,) + piece)
        for s in range(bits - 1):
            stage_bufs.append(v((len(stage_masks(order, s, pairs)),) + tail))
    n_sems = sem_count(n_dp, n_seq, lanes_in)
    vmem = pl.BlockSpec(memory_space=pltpu.VMEM)
    hbm = pl.BlockSpec(memory_space=pltpu.HBM)
    cot = cotangent[0]
    layer, mlp_sum, filt, small = pl.pallas_call(
        lambda *refs: mega_kernel(n_dp, n_seq, lanes_in, *refs),
        out_shape=(
            jax.ShapeDtypeStruct(cot.shape, BF16),
            jax.ShapeDtypeStruct((part, cols), F32),
            jax.ShapeDtypeStruct((n_dp,) + piece, BF16),
            jax.ShapeDtypeStruct((2, rows_half, channels), F32),
        ),
        in_specs=[vmem] * 6 + [hbm] * 3,
        out_specs=[vmem] * 4,
        scratch_shapes=[
            v(table.shape),
            v(mlp_weights.shape),
            v(cot.shape),
            v((lanes_in, n_seq, own_rows, wide)),
            v((n_seq,) + tokens.shape, jnp.int32),
            v((channels, block_len), F32),
            v((2, channels, block_len)),
            v((channels, two), F32),
            v((channels, two)),
            v((channels, two), F32),
            v((channels, two), F32),
            v((mlp_weights.shape[0] // 3, two), F32),
        ]
        + [v((2, pairs, size, channels)) for size in sizes]
        + [v((pairs, size, channels)) for size in sizes]
        + [v((pairs, size, channels)) for size in sizes]
        + [v((2, pairs, n_seq) + piece), v((pairs, n_seq) + piece), v((pairs, n_seq) + piece)]
        + [v((n_seq, size, cols)) for size in sizes]
        + [v((n_seq - 1, size, cols)) for size in sizes]
        + [
            v((n_seq - 1,) + piece),
            v(piece),
            v((2, rows_half, channels), F32),
            v((bits, rows_half, channels), F32),
            v((bits, rows_half, channels), F32),
            v((n_seq, rows_half, channels), F32),
        ]
        + stage_bufs
        + [
            pltpu.SemaphoreType.DMA((3,)),
            pltpu.SemaphoreType.DMA((n_sems,)),
            pltpu.SemaphoreType.DMA((n_sems,)),
        ],
        compiler_params=pltpu.CompilerParams(
            collective_id=0, has_side_effects=True, vmem_limit_bytes=44 * 2**20
        ),
        name="mega",
    )(tokens, embedding, gain_in, gain_mid, taps, long_filter, table, mlp_weights, cot)
    layer_out, grad_emb, grad_gain, grad_conv, grad_filter, grad_mid, grad_mlp = pl.pallas_call(
        lambda *refs: finish_kernel(n_taps, *refs),
        out_shape=(
            jax.ShapeDtypeStruct(cot.shape, BF16),
            jax.ShapeDtypeStruct(embedding.shape, F32),
            jax.ShapeDtypeStruct(gain_in.shape, F32),
            jax.ShapeDtypeStruct(taps.shape, F32),
            jax.ShapeDtypeStruct(long_filter.shape, F32),
            jax.ShapeDtypeStruct(gain_mid.shape, F32),
            jax.ShapeDtypeStruct((part, cols), F32),
        ),
        in_specs=[vmem] * 7,
        out_specs=[vmem] * 7,
        name="finish",
    )(layer, mlp_sum, filt, small, embedding, gain_in, taps)
    return layer_out[None], grad_emb, grad_gain, grad_conv.T, grad_filter, grad_mid, grad_mlp


def solution(mesh):
    placed = (P("dp", "seq"), P(), P(), P(), P("seq", None), P(), P(), P("dp", None, "seq"))
    return jax.shard_map(
        on_device,
        mesh=mesh,
        in_specs=placed,
        out_specs=(P("dp", None, "seq"), P(), P(), P(), P("seq", None), P(), P("dp", "seq")),
        check_vma=False,
    )
```

```python
import jax
import jax.numpy as jnp
import numpy as np
from jax import lax
from jax.experimental import pallas as pl
from jax.experimental.pallas import tpu as pltpu
from jax.sharding import PartitionSpec as P

F32 = jnp.float32
BF16 = jnp.bfloat16


def dct_table(length):
    freq = np.arange(length)[:, None]
    place = np.arange(length)[None, :]
    phase = (2 * place + 1) * freq % (4 * length)
    weight = np.where(freq == 0, np.sqrt(1.0 / length), np.sqrt(2.0 / length))
    return (weight * np.cos(np.pi * phase / (2 * length))).astype(np.float32).astype(BF16)


def dot(a, b, dims):
    return lax.dot_general(a, b, (dims, ((), ())), preferred_element_type=F32)


MESH = pl.DeviceIdType.MESH
TILE = 16


def flip(index, mask):
    bit = 1
    while bit <= mask:
        if mask & bit:
            index = index + bit * (1 - 2 * lax.rem(index // bit, 2))
        bit *= 2
    return index


def chunk_rows(part):
    units = part // TILE
    sizes = [TILE * ((units + 3 - i) // 4) for i in range(4)]
    sizes[3] += part - sum(sizes)
    return sizes


def stage_masks(order, stage, count):
    sent = [
        r
        for r in range(count)
        if (r >> order[stage]) & 1 and not any((r >> o) & 1 for o in order[:stage])
    ]
    return sorted(sent, key=lambda r: [-((r >> o) & 1) for o in order[stage + 1 :]])


class Sems:
    def __init__(self, send, recv):
        self.send, self.recv, self.used, self.started = send, recv, 0, []

    def take(self, count=1):
        first = self.used
        self.used += count
        return first

    def copy(self, index, src, dst, peer):
        return pltpu.make_async_remote_copy(
            src_ref=src,
            dst_ref=dst,
            send_sem=self.send.at[index],
            recv_sem=self.recv.at[index],
            device_id=peer,
            device_id_type=MESH,
        )

    def start(self, index, src, dst, peer):
        copy = self.copy(index, src, dst, peer)
        copy.start()
        self.started.append(copy)

    def arrived(self, index, dst, peer):
        self.copy(index, dst, dst, peer).wait_recv()

    def drain(self):
        for copy in self.started:
            copy.wait_send()


class Stream:
    def __init__(self, sems, order, place, recs):
        self.sems, self.order, self.place, self.recs = sems, order, place, recs
        self.count = 2 ** len(order)
        self.base = [sems.take(len(stage_masks(order, s, self.count))) for s in range(len(order))]

    def send_one(self, stage, mask, dp, sq):
        slot = stage_masks(self.order, stage, self.count).index(mask)
        peer = (flip(dp, 2 << self.order[stage]), sq)
        self.sems.start(
            self.base[stage] + slot, self.place(flip(dp // 2, mask)), self.recs[stage].at[slot], peer
        )

    def send_first(self, dp, sq, which):
        masks = stage_masks(self.order, 0, self.count)
        self.send_one(0, masks[which], dp, sq)

    def take_in(self, stage, dp, sq):
        for slot, mask in enumerate(stage_masks(self.order, stage, self.count)):
            kept = mask ^ (1 << self.order[stage])
            self.sems.arrived(self.base[stage] + slot, self.recs[stage].at[slot], (dp, sq))
            ref = self.place(flip(dp // 2, kept))
            ref[...] = (ref[...].astype(F32) + self.recs[stage][slot].astype(F32)).astype(BF16)
            if stage + 1 < len(self.order) and (kept >> self.order[stage + 1]) & 1:
                self.send_one(stage + 1, kept, dp, sq)


def sem_count(n_dp, n_seq, lanes_in):
    far, pairs = n_seq - 1, n_dp // 2
    bits = n_dp.bit_length() - 1
    return 2 * far + far * lanes_in + 4 * pairs + 2 + 6 * (pairs - 1) + bits + far + 6 * far + n_dp


def mega_kernel(
    n_dp, n_seq, lanes_in,
    ids, emb, gin, gmid, taps_in, shard, table_h, mlp_h, cot_h,
    out, mlp_out, filt_out, small_out,
    table, mlp, cot, gath, all_ids, full, spec_ref, level_ref, normed_ref, d_normed_ref, down_ref, d_act_ref,
    g0, g1, g2, g3, r0, r1, r2, r3, m0, m1, m2, m3,
    gf, rf, mf, z0, z1, z2, z3, y0, y1, y2, y3, yf, mine,
    sm, s_rec, s_acc, zs_rec,
    *rest,
):
    bits = n_dp.bit_length() - 1
    pairs = n_dp // 2
    stage_bufs = list(rest[: 6 * (bits - 1)])
    load_sem, send, recv = rest[6 * (bits - 1) :]
    sems = Sems(send, recv)
    grads, recs0, sums = (g0, g1, g2, g3), (r0, r1, r2, r3), (m0, m1, m2, m3)
    z_out, z_in = (z0, z1, z2, z3), (y0, y1, y2, y3)
    own_rows, block_len = shard.shape
    channels = own_rows * n_seq
    local_len = ids.shape[1]
    hidden = mlp.shape[0] // 3
    n_taps = taps_in.shape[0]
    half = 4 * n_taps
    part = mlp.shape[0] // n_dp
    sizes = chunk_rows(part)
    dp, sq = lax.axis_index("dp"), lax.axis_index("seq")
    core = lax.rem(dp, 2)
    me_q = dp // 2
    mate = (flip(dp, 1), sq)
    here = (dp, sq)
    wide = block_len // lanes_in
    lane_at = lax.rem(dp, lanes_in)

    loads = [
        pltpu.make_async_copy(table_h, table, load_sem.at[0]),
        pltpu.make_async_copy(cot_h, cot, load_sem.at[1]),
        pltpu.make_async_copy(mlp_h, mlp, load_sem.at[2]),
    ]
    for load in loads:
        load.start()
    barrier = pltpu.get_barrier_semaphore()
    for mask in range(1, n_dp):
        pl.semaphore_signal(barrier, inc=1, device_id=(flip(dp, mask), sq), device_id_type=MESH)
    for mask in range(1, n_seq):
        pl.semaphore_signal(barrier, inc=1, device_id=(dp, flip(sq, mask)), device_id_type=MESH)
    for p in range(lanes_in):
        gath[p, sq] = shard[:, p * wide : (p + 1) * wide].astype(BF16)
    all_ids[sq] = ids[...]
    pl.semaphore_wait(barrier, n_dp + n_seq - 2)

    id_base = sems.take(n_seq - 1)
    z_base = sems.take(n_seq - 1)
    for k in range(1, n_seq):
        to = (dp, flip(sq, k))
        sems.start(id_base + k - 1, ids, all_ids.at[sq], to)
        sems.start(z_base + k - 1, gath.at[lane_at, sq], gath.at[lane_at, sq], to)

    pad = 128 - 6 - n_taps
    rows_all = jnp.concatenate(
        [
            emb[...],
            gin[...].reshape(1, channels),
            gmid[...].reshape(1, channels),
            taps_in[...],
            jnp.zeros((pad, channels), F32),
        ],
        0,
    )
    packed = rows_all.T
    emb_cols, gain_in, gain_mid = packed[:, :4], packed[:, 4:5], packed[:, 5:6]
    taps = packed[:, 6 : 6 + n_taps]
    base_scale = lax.rsqrt(jnp.mean(emb_cols * emb_cols, axis=0, keepdims=True) + 1e-6)
    base_norm = (emb_cols * base_scale * gain_in).astype(BF16).astype(F32)
    lane = lax.broadcasted_iota(jnp.int32, (channels, half), 1)
    tap_part = jnp.zeros((channels, half), F32)
    base_part = jnp.zeros((channels, half), F32)
    for k in range(n_taps):
        tap_part = jnp.where(lane // 4 == k, taps[:, k : k + 1], tap_part)
    for a in range(4):
        base_part = jnp.where(lane % 4 == a, base_norm[:, a : a + 1], base_part)
    kmer = (tap_part * base_part).astype(BF16)
    turn = jnp.where(
        lax.broadcasted_iota(jnp.int32, (channels, channels), 0)
        + lax.broadcasted_iota(jnp.int32, (channels, channels), 1)
        == channels - 1,
        1.0,
        0.0,
    ).astype(BF16)
    loads[1].wait()
    turned = dot(turn, cot[channels:, :], ((1,), (0,))).astype(BF16)
    back = jnp.concatenate([cot[:channels, :], turned], 1)

    masks = [*range(2, lanes_in, 2)]
    near = [0] + masks if lanes_in > 1 else []
    far_base = sems.take((n_seq - 1) * len(masks))
    mate_base = sems.take((n_seq - 1) * len(near))

    def to_mate(k, n):
        piece = gath.at[flip(lane_at, near[n]), flip(sq, k)]
        sems.start(mate_base + (k - 1) * len(near) + n, piece, piece, mate)

    for k in range(1, n_seq):
        piece = gath.at[lane_at, flip(sq, k)]
        sems.arrived(z_base + k - 1, piece, here)
        for n, mask in enumerate(masks):
            sems.start(far_base + (k - 1) * len(masks) + n, piece, piece, (flip(dp, mask), sq))
        if near:
            to_mate(k, 0)
    for k in range(1, n_seq):
        sems.arrived(id_base + k - 1, all_ids.at[flip(sq, k)], here)

    per_block = block_len // local_len
    first = sq // per_block * per_block
    last = first + per_block - 1
    offset = pl.multiple_of((sq - first) * local_len, local_len)
    edge = 128
    before = jnp.where(first > 0, all_ids[jnp.maximum(first - 1, 0)][:, local_len - edge :], 4)
    after = jnp.where(last < n_seq - 1, all_ids[jnp.minimum(last + 1, n_seq - 1)][:, :edge], 4)
    row = jnp.concatenate([before] + [all_ids[first + j] for j in range(per_block)] + [after], 1)
    width = block_len + 2 * edge
    spread = jnp.broadcast_to(row, (8, width))
    sub = lax.broadcasted_iota(jnp.int32, (8, block_len), 0)
    tiles = []
    for s in range(2):
        for k in range(0, n_taps, 2):
            shifts = [(k + i) if s == 0 else (width - k - i) % width for i in range(2)]
            moved = [(pltpu.roll(spread, sh, 1) if sh else spread)[:, edge : edge + block_len] for sh in shifts]
            picked = jnp.where(sub < 4, moved[0], moved[1])
            want = sub % 4 if s == 0 else 3 - sub % 4
            tiles.append(jnp.where(picked == want, 1.0, 0.0))
    hot = jnp.concatenate(tiles, 0).astype(BF16)
    loads[0].wait()
    hot_spec = dot(hot, table[...], ((1,), (0,))).astype(BF16)
    for s in range(2):
        spec_ref[s] = dot(kmer, hot_spec[s * half : (s + 1) * half], ((1,), (0,))).astype(BF16)
    loads[2].wait()
    d_act_ref[...] = dot(mlp[2 * hidden :, :], back, ((1,), (0,)))

    for k in range(1, n_seq):
        for n, mask in enumerate(masks):
            piece = gath.at[flip(lane_at, mask), flip(sq, k)]
            sems.arrived(far_base + (k - 1) * len(masks) + n, piece, here)
            to_mate(k, n + 1)
    for k in range(1, n_seq):
        for n in range(len(near)):
            piece = gath.at[flip(lane_at, near[n] + 1), flip(sq, k)]
            sems.arrived(mate_base + (k - 1) * len(near) + n, piece, here)

    for p in range(lanes_in):
        full[:, p * wide : (p + 1) * wide] = gath[p].astype(F32).reshape(channels, wide)
    own = ids[...]
    q_own = table[pl.ds(offset, local_len), :]
    for s in range(2):
        scaled = (full[...] * spec_ref[s].astype(F32)).astype(BF16)
        mine_ids = own if s == 0 else 3 - own
        level = dot(scaled, q_own, ((1,), (1,)))
        residual = jnp.zeros((channels, local_len), F32)
        for a in range(4):
            residual = jnp.where(mine_ids == a, emb_cols[:, a : a + 1], residual)
        level_ref[:, s * local_len : (s + 1) * local_len] = level + residual
    level = level_ref[...]
    mid_scale = lax.rsqrt(jnp.mean(level * level, axis=0, keepdims=True) + 1e-6)
    normed_ref[...] = (level * mid_scale * gain_mid).astype(BF16)
    normed = normed_ref[...]

    edges = []
    for i in range(n_dp):
        at = i * part
        for c in range(4):
            edges.append((at, at + sizes[c], i, c))
            at += sizes[c]
    filled = {(i, c): 0 for i in range(n_dp) for c in range(4)}
    core_base = sems.take(4 * pairs)
    gone = set()

    def put(start, value):
        for lo, hi, i, c in edges:
            a, b = max(lo, start), min(hi, start + value.shape[0])
            if a < b:
                grads[c][i % 2, i // 2, a - lo : b - lo, :] = value[a - start : b - start, :]
                filled[i, c] += b - a

    def swap_done():
        for c in range(4):
            for q in range(pairs):
                if (c, q) not in gone and filled[2 * q, c] == sizes[c] and filled[2 * q + 1, c] == sizes[c]:
                    gone.add((c, q))
                    sems.start(core_base + c * pairs + q, grads[c].at[1 - core, q], recs0[c].at[q], mate)

    tile = 256 if hidden % 256 == 0 else hidden
    for t in range(hidden // tile):
        a0, u0, w0 = t * tile, hidden + t * tile, 2 * hidden + t * tile
        w_gate, w_up, w_down = mlp[a0 : a0 + tile, :], mlp[u0 : u0 + tile, :], mlp[w0 : w0 + tile, :]
        gate = dot(w_gate, normed, ((1,), (0,)))
        up = dot(w_up, normed, ((1,), (0,)))
        d_act = d_act_ref[a0 : a0 + tile, :]
        sig = jax.nn.sigmoid(gate)
        silu = gate * sig
        act = (silu * up).astype(BF16)
        d_gate = (d_act * up * (sig + silu * (1.0 - sig))).astype(BF16)
        d_up = (d_act * silu).astype(BF16)
        for start, left, right in ((a0, d_gate, normed), (u0, d_up, normed), (w0, act, back)):
            put(start, dot(left, right, ((1,), (1,))).astype(BF16))
        swap_done()
        down = dot(w_down, act, ((0,), (0,)))
        down_ref[...] = down if t == 0 else down_ref[...] + down
        d_part = dot(w_gate, d_gate, ((0,), (0,))) + dot(w_up, d_up, ((0,), (0,)))
        d_normed_ref[...] = d_part if t == 0 else d_normed_ref[...] + d_part

    order_a = [*range(bits - 1)]
    order_b = [*range(1, bits - 1)] + [0] if bits > 1 else []
    streams = []
    for c in range(4):
        recs = [stage_bufs[c * (bits - 1) + s] for s in range(bits - 1)]
        streams.append(Stream(sems, order_b if c % 2 else order_a, lambda q, c=c: sums[c].at[q], recs))
    split = n_seq // 2
    for c in range(2):
        recs = [stage_bufs[(4 + c) * (bits - 1) + s] for s in range(bits - 1)]
        lo, hi = (0, split) if c == 0 else (split, n_seq)
        streams.append(
            Stream(sems, order_b if c % 2 else order_a, lambda q, lo=lo, hi=hi: mf.at[q, pl.ds(lo, hi - lo)], recs)
        )
    n_first = len(stage_masks(order_a, 0, pairs)) if bits > 1 else 0

    def open_pair(lead):
        for c in (lead, lead + 1):
            for q in range(pairs):
                sems.arrived(core_base + c * pairs + q, recs0[c].at[q], here)
                sums[c][q] = (grads[c][core, q].astype(F32) + recs0[c][q].astype(F32)).astype(BF16)
        for which in range(n_first):
            for c in (lead, lead + 1):
                streams[c].send_first(dp, sq, which)

    def middle(lead):
        for stage in range(bits - 1):
            for c in (lead, lead + 1):
                streams[c].take_in(stage, dp, sq)

    cols = channels // n_seq
    zm_base = sems.take(4 * (n_seq - 1))

    def across(c):
        total = sums[c][me_q]
        for j in range(n_seq):
            z_out[c][j] = total[:, j * cols : (j + 1) * cols]
        for k in range(1, n_seq):
            sems.start(
                zm_base + c * (n_seq - 1) + k - 1, z_out[c].at[flip(sq, k)], z_in[c].at[k - 1], (dp, flip(sq, k))
            )

    open_pair(0)

    mid_level = level_ref[...]
    combined = (mid_level + down_ref[...]).astype(BF16)
    out[:channels, :] = combined[:, :local_len]
    out[channels:, :] = dot(turn, combined[:, local_len:], ((1,), (0,))).astype(BF16)
    unit = mid_level * mid_scale
    d_normed = d_normed_ref[...]
    mid_grad = d_normed * unit
    d_unit = d_normed * gain_mid
    d_level = back.astype(F32) + mid_scale * (d_unit - unit * jnp.mean(d_unit * unit, axis=0, keepdims=True))
    d_bf = d_level.astype(BF16)
    d_low = (d_level - d_bf.astype(F32)).astype(BF16)
    both = jnp.concatenate([own, 3 - own], 1)
    sub8 = lax.broadcasted_iota(jnp.int32, (8, 2 * local_len), 0)
    own_hot = jnp.where(sub8 == both, 1.0, 0.0).astype(BF16)
    ones = jnp.ones((8, 2 * local_len), BF16)
    m_bf = mid_grad.astype(BF16)
    m_low = (mid_grad - m_bf.astype(F32)).astype(BF16)
    base_part_sum = dot(own_hot, d_bf, ((1,), (1,))) + dot(own_hot, d_low, ((1,), (1,)))
    mid_part_sum = dot(ones, m_bf, ((1,), (1,))) + dot(ones, m_low, ((1,), (1,)))

    open_pair(2)

    grad_filter = jnp.zeros((channels, block_len), F32)
    kmer_sum = jnp.zeros((half, channels), F32)
    for s in range(2):
        d_scaled = dot(d_bf[:, s * local_len : (s + 1) * local_len], q_own, ((1,), (0,)))
        grad_filter = grad_filter + d_scaled * spec_ref[s].astype(F32)
        d_spec = (full[...] * d_scaled).astype(BF16)
        kmer_sum = kmer_sum + dot(hot_spec[s * half : (s + 1) * half], d_spec, ((1,), (1,)))
    grad_filter = grad_filter.astype(BF16)
    groups = n_dp // lanes_in
    piece_rows = own_rows // groups
    for i in range(n_dp):
        block = grad_filter[:, i % lanes_in * wide : (i % lanes_in + 1) * wide]
        for j in range(n_seq):
            top = j * own_rows + i // lanes_in * piece_rows
            gf[i % 2, i // 2, j] = block[top : top + piece_rows, :]
    rows_half = sm.shape[1]
    joined = jnp.concatenate([kmer_sum, base_part_sum, mid_part_sum], 0)
    sm[0] = joined[:rows_half]
    sm[1] = joined[rows_half:]
    f_base, s_base = sems.take(), sems.take(bits)
    sems.start(f_base, gf.at[1 - core], rf, mate)
    sems.start(s_base, sm.at[1 - core], s_rec.at[0], mate)

    middle(0)
    across(0)
    across(1)

    sems.arrived(f_base, rf, here)
    for q in range(pairs):
        mf[q] = (gf[core, q].astype(F32) + rf[q].astype(F32)).astype(BF16)
    for which in range(n_first):
        for c in (4, 5):
            streams[c].send_first(dp, sq, which)
    for b in range(bits):
        sems.arrived(s_base + b, s_rec.at[b], here)
        s_acc[b] = (sm[core] if b == 0 else s_acc[b - 1]) + s_rec[b]
        if b + 1 < bits:
            sems.start(s_base + b + 1, s_acc.at[b], s_rec.at[b + 1], (flip(dp, 2 << b), sq))
    zs_base = sems.take(n_seq - 1)
    zs_rec[sq] = s_acc[bits - 1]
    for k in range(1, n_seq):
        sems.start(zs_base + k - 1, s_acc.at[bits - 1], zs_rec.at[sq], (dp, flip(sq, k)))

    middle(4)
    zf_base = sems.take(n_seq - 1)
    for k in range(1, n_seq):
        sems.start(zf_base + k - 1, mf.at[me_q, flip(sq, k)], yf.at[k - 1], (dp, flip(sq, k)))
    middle(2)
    across(2)
    across(3)

    for k in range(1, n_seq):
        sems.arrived(zs_base + k - 1, zs_rec.at[flip(sq, k)], here)
    total = zs_rec[0]
    for j in range(1, n_seq):
        total = total + zs_rec[j]
    small_out[core] = total
    back_base = sems.take()
    sems.start(back_base, small_out.at[core], small_out.at[core], mate)

    total = mf[me_q, sq].astype(F32)
    for k in range(1, n_seq):
        sems.arrived(zf_base + k - 1, yf.at[k - 1], here)
        total = total + yf[k - 1].astype(F32)
    filt_out[dp] = total.astype(BF16)
    ring_base = sems.take(n_dp - 1)
    for mask in range(1, n_dp):
        sems.start(ring_base + mask - 1, filt_out.at[dp], filt_out.at[dp], (flip(dp, mask), sq))
    at = 0
    for c in range(4):
        total = z_out[c][sq].astype(F32)
        for k in range(1, n_seq):
            sems.arrived(zm_base + c * (n_seq - 1) + k - 1, z_in[c].at[k - 1], here)
            total = total + z_in[c][k - 1].astype(F32)
        mlp_out[at : at + sizes[c], :] = total
        at += sizes[c]
    sems.arrived(back_base, small_out.at[1 - core], here)
    for mask in range(1, n_dp):
        sems.arrived(ring_base + mask - 1, filt_out.at[flip(dp, mask)], here)
    sems.drain()


def finish_kernel(
    n_taps, layer, mlp_sum, filt, small, embedding, gain_in, taps,
    layer_out, grad_emb, grad_gain, grad_conv, filt_out, grad_mid, mlp_out,
):
    layer_out[...] = layer[...]
    mlp_out[...] = mlp_sum[...]
    n_dp, rows, wide = filt.shape
    lanes_in = filt_out.shape[1] // wide
    for i in range(n_dp):
        top, left = i // lanes_in * rows, i % lanes_in * wide
        filt_out[top : top + rows, left : left + wide] = filt[i].astype(F32)
    channels = embedding.shape[1]
    sums = jnp.concatenate([small[0], small[1]], 0)
    emb = embedding[...]
    gain = gain_in[...].reshape(1, channels)
    base_scale = lax.rsqrt(jnp.mean(emb * emb, axis=1, keepdims=True) + 1e-6)
    unit = emb * base_scale
    base_norm = (unit * gain).astype(BF16).astype(F32)
    d_norm = jnp.zeros(emb.shape, F32)
    for k in range(n_taps):
        part = sums[4 * k : 4 * k + 4, :]
        d_norm = d_norm + part * taps[k : k + 1, :]
        grad_conv[k : k + 1, :] = jnp.sum(part * base_norm, axis=0, keepdims=True)
    grad_gain[...] = jnp.sum(d_norm * unit, axis=0)
    d_unit = d_norm * gain
    base_sum = sums[4 * n_taps : 4 * n_taps + 4, :]
    grad_emb[...] = base_sum + base_scale * (d_unit - unit * jnp.mean(d_unit * unit, axis=1, keepdims=True))
    grad_mid[...] = sums[4 * n_taps + 8 : 4 * n_taps + 9, :].reshape(channels)


def on_device(tokens, embedding, gain_in, conv_taps, long_filter, gain_mid, mlp_weights, cotangent):
    n_dp, n_seq = lax.axis_size("dp"), lax.axis_size("seq")
    own_rows, block_len = long_filter.shape
    channels = own_rows * n_seq
    local_len = tokens.shape[1]
    lanes_in = n_dp
    while block_len % (lanes_in * 128):
        lanes_in //= 2
    wide = block_len // lanes_in
    table = jnp.asarray(dct_table(block_len).T)
    taps = conv_taps.T
    n_taps = taps.shape[0]
    pairs, bits = n_dp // 2, n_dp.bit_length() - 1
    part = mlp_weights.shape[0] // n_dp
    sizes = chunk_rows(part)
    cols = channels // n_seq
    piece = (own_rows // (n_dp // lanes_in), wide)
    rows_half = (4 * n_taps + 16) // 2
    orders = [[*range(bits - 1)], [*range(1, bits - 1)] + [0] if bits > 1 else []]
    two = 2 * local_len

    def v(shape, dtype=BF16):
        return pltpu.VMEM(shape, dtype)

    stage_bufs = []
    for c in range(6):
        order = orders[c % 2]
        split = n_seq // 2
        tail = (sizes[c], channels) if c < 4 else ((split if c == 4 else n_seq - split,) + piece)
        for s in range(bits - 1):
            stage_bufs.append(v((len(stage_masks(order, s, pairs)),) + tail))
    n_sems = sem_count(n_dp, n_seq, lanes_in)
    vmem = pl.BlockSpec(memory_space=pltpu.VMEM)
    hbm = pl.BlockSpec(memory_space=pltpu.HBM)
    cot = cotangent[0]
    layer, mlp_sum, filt, small = pl.pallas_call(
        lambda *refs: mega_kernel(n_dp, n_seq, lanes_in, *refs),
        out_shape=(
            jax.ShapeDtypeStruct(cot.shape, BF16),
            jax.ShapeDtypeStruct((part, cols), F32),
            jax.ShapeDtypeStruct((n_dp,) + piece, BF16),
            jax.ShapeDtypeStruct((2, rows_half, channels), F32),
        ),
        in_specs=[vmem] * 6 + [hbm] * 3,
        out_specs=[vmem] * 4,
        scratch_shapes=[
            v(table.shape),
            v(mlp_weights.shape),
            v(cot.shape),
            v((lanes_in, n_seq, own_rows, wide)),
            v((n_seq,) + tokens.shape, jnp.int32),
            v((channels, block_len), F32),
            v((2, channels, block_len)),
            v((channels, two), F32),
            v((channels, two)),
            v((channels, two), F32),
            v((channels, two), F32),
            v((mlp_weights.shape[0] // 3, two), F32),
        ]
        + [v((2, pairs, size, channels)) for size in sizes]
        + [v((pairs, size, channels)) for size in sizes]
        + [v((pairs, size, channels)) for size in sizes]
        + [v((2, pairs, n_seq) + piece), v((pairs, n_seq) + piece), v((pairs, n_seq) + piece)]
        + [v((n_seq, size, cols)) for size in sizes]
        + [v((n_seq - 1, size, cols)) for size in sizes]
        + [
            v((n_seq - 1,) + piece),
            v(piece),
            v((2, rows_half, channels), F32),
            v((bits, rows_half, channels), F32),
            v((bits, rows_half, channels), F32),
            v((n_seq, rows_half, channels), F32),
        ]
        + stage_bufs
        + [
            pltpu.SemaphoreType.DMA((3,)),
            pltpu.SemaphoreType.DMA((n_sems,)),
            pltpu.SemaphoreType.DMA((n_sems,)),
        ],
        compiler_params=pltpu.CompilerParams(
            collective_id=0, has_side_effects=True, vmem_limit_bytes=62 * 2**20
        ),
        name="mega",
    )(tokens, embedding, gain_in, gain_mid, taps, long_filter, table, mlp_weights, cot)
    layer_out, grad_emb, grad_gain, grad_conv, grad_filter, grad_mid, grad_mlp = pl.pallas_call(
        lambda *refs: finish_kernel(n_taps, *refs),
        out_shape=(
            jax.ShapeDtypeStruct(cot.shape, BF16),
            jax.ShapeDtypeStruct(embedding.shape, F32),
            jax.ShapeDtypeStruct(gain_in.shape, F32),
            jax.ShapeDtypeStruct(taps.shape, F32),
            jax.ShapeDtypeStruct(long_filter.shape, F32),
            jax.ShapeDtypeStruct(gain_mid.shape, F32),
            jax.ShapeDtypeStruct((part, cols), F32),
        ),
        in_specs=[vmem] * 7,
        out_specs=[vmem] * 7,
        compiler_params=pltpu.CompilerParams(vmem_limit_bytes=62 * 2**20),
        name="finish",
    )(layer, mlp_sum, filt, small, embedding, gain_in, taps)
    return layer_out[None], grad_emb, grad_gain, grad_conv.T, grad_filter, grad_mid, grad_mlp


def solution(mesh):
    placed = (P("dp", "seq"), P(), P(), P(), P("seq", None), P(), P(), P("dp", None, "seq"))
    return jax.shard_map(
        on_device,
        mesh=mesh,
        in_specs=placed,
        out_specs=(P("dp", None, "seq"), P(), P(), P(), P("seq", None), P(), P("dp", "seq")),
        check_vma=False,
    )
```

```python
import math

import jax
import jax.numpy as jnp
import numpy as np
from jax import lax
from jax.experimental import pallas as pl
from jax.experimental.pallas import tpu as pltpu
from jax.sharding import PartitionSpec as P

F32 = jnp.float32
BF16 = jnp.bfloat16


def dct_table(length):
    freq = np.arange(length)[:, None]
    place = np.arange(length)[None, :]
    phase = (2 * place + 1) * freq % (4 * length)
    weight = np.where(freq == 0, np.sqrt(1.0 / length), np.sqrt(2.0 / length))
    return (weight * np.cos(np.pi * phase / (2 * length))).astype(np.float32).astype(BF16)


def dot(a, b, dims):
    return lax.dot_general(a, b, (dims, ((), ())), preferred_element_type=F32)


MESH = pl.DeviceIdType.MESH
N_TILES = 3


def flip(index, mask):
    bit = 1
    while bit <= mask:
        if mask & bit:
            index = index + bit * (1 - 2 * lax.rem(index // bit, 2))
        bit *= 2
    return index


def row_group(part, hidden):
    return math.gcd(part, hidden) // N_TILES


def color_rows(rows):
    return rows // 32 * 16 or 8


def pack_rows(rows, cols):
    spare = 128 - cols
    if spare <= 0 or cols % spare or rows % (8 * (cols // spare + 1)):
        return 0
    return rows * cols // 128


def pack(block):
    rows, cols = block.shape
    main = pack_rows(rows, cols)
    if not main:
        return block
    spare = 128 - cols
    rest = jnp.concatenate([block[main:, at : at + spare] for at in range(0, cols, spare)], 0)
    return jnp.concatenate([block[:main], rest], 1)


def unpack(block, rows, cols):
    main = pack_rows(rows, cols)
    if not main:
        return block
    rest = jnp.concatenate([block[at : at + rows - main, cols:] for at in range(0, main, rows - main)], 1)
    return jnp.concatenate([block[:, :cols], rest], 0)


def stage_masks(order, stage, count):
    sent = [
        r
        for r in range(count)
        if (r >> order[stage]) & 1 and not any((r >> o) & 1 for o in order[:stage])
    ]
    return sorted(sent, key=lambda r: [-((r >> o) & 1) for o in order[stage + 1 :]])


class Sems:
    def __init__(self, send, recv):
        self.send, self.recv, self.used, self.started = send, recv, 0, []

    def take(self, count=1):
        first = self.used
        self.used += count
        return first

    def copy(self, index, src, dst, peer):
        return pltpu.make_async_remote_copy(
            src_ref=src,
            dst_ref=dst,
            send_sem=self.send.at[index],
            recv_sem=self.recv.at[index],
            device_id=peer,
            device_id_type=MESH,
        )

    def start(self, index, src, dst, peer):
        copy = self.copy(index, src, dst, peer)
        copy.start()
        self.started.append(copy)

    def arrived(self, index, dst, peer):
        self.copy(index, dst, dst, peer).wait_recv()

    def drain(self):
        for copy in self.started:
            copy.wait_send()


class Stream:
    def __init__(self, sems, order, place, recs):
        self.sems, self.order, self.place, self.recs = sems, order, place, recs
        self.count = 2 ** len(order)
        self.base = [sems.take(len(stage_masks(order, s, self.count))) for s in range(len(order))]

    def send_one(self, stage, mask, dp, sq):
        slot = stage_masks(self.order, stage, self.count).index(mask)
        peer = (flip(dp, 2 << self.order[stage]), sq)
        self.sems.start(
            self.base[stage] + slot, self.place(flip(dp // 2, mask)), self.recs[stage].at[slot], peer
        )

    def send_first(self, dp, sq, which):
        masks = stage_masks(self.order, 0, self.count)
        self.send_one(0, masks[which], dp, sq)

    def take_in(self, stage, dp, sq):
        for slot, mask in enumerate(stage_masks(self.order, stage, self.count)):
            kept = mask ^ (1 << self.order[stage])
            self.sems.arrived(self.base[stage] + slot, self.recs[stage].at[slot], (dp, sq))
            ref = self.place(flip(dp // 2, kept))
            ref[...] = (ref[...].astype(F32) + self.recs[stage][slot].astype(F32)).astype(BF16)
            if stage + 1 < len(self.order) and (kept >> self.order[stage + 1]) & 1:
                self.send_one(stage + 1, kept, dp, sq)


def sem_count(n_dp, n_seq, lanes_in):
    far, pairs = n_seq - 1, n_dp // 2
    bits = n_dp.bit_length() - 1
    return 2 * far + far * lanes_in + N_TILES + 2 + 8 * (pairs - 1) + bits + far + 6 * far + n_dp


def mega_kernel(
    n_dp, n_seq, lanes_in,
    ids, emb, gin, gmid, taps_in, shard, table_h, mlp_h, cot_h,
    out, mlp_out, filt_out, small_out,
    table, mlp, cot, gath, all_ids, full, spec_ref, level_ref, normed_ref, d_normed_ref, down_ref, d_act_ref,
    grads, recs0, sums, z_out, z_in, keep, gf, rf, mf, yf,
    sm, s_rec, s_acc, zs_rec,
    *rest,
):
    bits = n_dp.bit_length() - 1
    pairs = n_dp // 2
    stage_bufs = list(rest[: 8 * (bits - 1)])
    load_sem, send, recv = rest[8 * (bits - 1) :]
    sems = Sems(send, recv)
    own_rows, block_len = shard.shape
    channels = own_rows * n_seq
    local_len = ids.shape[1]
    hidden = mlp.shape[0] // 3
    n_taps = taps_in.shape[0]
    half = 4 * n_taps
    part = mlp.shape[0] // n_dp
    group = row_group(part, hidden)
    span = N_TILES * group
    chunk = part // N_TILES
    dp, sq = lax.axis_index("dp"), lax.axis_index("seq")
    core = lax.rem(dp, 2)
    me_q = dp // 2
    mate = (flip(dp, 1), sq)
    here = (dp, sq)
    wide = block_len // lanes_in
    lane_at = lax.rem(dp, lanes_in)

    loads = [
        pltpu.make_async_copy(table_h, table, load_sem.at[0]),
        pltpu.make_async_copy(cot_h, cot, load_sem.at[1]),
        pltpu.make_async_copy(mlp_h, mlp, load_sem.at[2]),
    ]
    for load in loads:
        load.start()
    barrier = pltpu.get_barrier_semaphore()
    for mask in range(1, n_dp):
        pl.semaphore_signal(barrier, inc=1, device_id=(flip(dp, mask), sq), device_id_type=MESH)
    for mask in range(1, n_seq):
        pl.semaphore_signal(barrier, inc=1, device_id=(dp, flip(sq, mask)), device_id_type=MESH)
    for p in range(lanes_in):
        gath[p, sq] = shard[:, p * wide : (p + 1) * wide].astype(BF16)
    all_ids[sq] = ids[...]
    pl.semaphore_wait(barrier, n_dp + n_seq - 2)

    id_base = sems.take(n_seq - 1)
    z_base = sems.take(n_seq - 1)
    for k in range(1, n_seq):
        to = (dp, flip(sq, k))
        sems.start(id_base + k - 1, ids, all_ids.at[sq], to)
        sems.start(z_base + k - 1, gath.at[lane_at, sq], gath.at[lane_at, sq], to)

    pad = 128 - 6 - n_taps
    rows_all = jnp.concatenate(
        [
            emb[...],
            gin[...].reshape(1, channels),
            gmid[...].reshape(1, channels),
            taps_in[...],
            jnp.zeros((pad, channels), F32),
        ],
        0,
    )
    packed = rows_all.T
    emb_cols, gain_in, gain_mid = packed[:, :4], packed[:, 4:5], packed[:, 5:6]
    taps = packed[:, 6 : 6 + n_taps]
    base_scale = lax.rsqrt(jnp.mean(emb_cols * emb_cols, axis=0, keepdims=True) + 1e-6)
    base_norm = (emb_cols * base_scale * gain_in).astype(BF16).astype(F32)
    lane = lax.broadcasted_iota(jnp.int32, (channels, half), 1)
    tap_part = jnp.zeros((channels, half), F32)
    base_part = jnp.zeros((channels, half), F32)
    for k in range(n_taps):
        tap_part = jnp.where(lane // 4 == k, taps[:, k : k + 1], tap_part)
    for a in range(4):
        base_part = jnp.where(lane % 4 == a, base_norm[:, a : a + 1], base_part)
    kmer = (tap_part * base_part).astype(BF16)
    turn = jnp.where(
        lax.broadcasted_iota(jnp.int32, (channels, channels), 0)
        + lax.broadcasted_iota(jnp.int32, (channels, channels), 1)
        == channels - 1,
        1.0,
        0.0,
    ).astype(BF16)
    loads[1].wait()
    turned = dot(turn, cot[channels:, :], ((1,), (0,))).astype(BF16)
    back = jnp.concatenate([cot[:channels, :], turned], 1)

    masks = [*range(2, lanes_in, 2)]
    near = [0] + masks if lanes_in > 1 else []
    far_base = sems.take((n_seq - 1) * len(masks))
    mate_base = sems.take((n_seq - 1) * len(near))

    def to_mate(k, n):
        piece = gath.at[flip(lane_at, near[n]), flip(sq, k)]
        sems.start(mate_base + (k - 1) * len(near) + n, piece, piece, mate)

    for k in range(1, n_seq):
        piece = gath.at[lane_at, flip(sq, k)]
        sems.arrived(z_base + k - 1, piece, here)
        for n, mask in enumerate(masks):
            sems.start(far_base + (k - 1) * len(masks) + n, piece, piece, (flip(dp, mask), sq))
        if near:
            to_mate(k, 0)
    for k in range(1, n_seq):
        sems.arrived(id_base + k - 1, all_ids.at[flip(sq, k)], here)

    per_block = block_len // local_len
    first = sq // per_block * per_block
    last = first + per_block - 1
    offset = pl.multiple_of((sq - first) * local_len, local_len)
    edge = 128
    before = jnp.where(first > 0, all_ids[jnp.maximum(first - 1, 0)][:, local_len - edge :], 4)
    after = jnp.where(last < n_seq - 1, all_ids[jnp.minimum(last + 1, n_seq - 1)][:, :edge], 4)
    row = jnp.concatenate([before] + [all_ids[first + j] for j in range(per_block)] + [after], 1)
    width = block_len + 2 * edge
    spread = jnp.broadcast_to(row, (8, width))
    sub = lax.broadcasted_iota(jnp.int32, (8, block_len), 0)
    tiles = []
    for s in range(2):
        for k in range(0, n_taps, 2):
            shifts = [(k + i) if s == 0 else (width - k - i) % width for i in range(2)]
            moved = [(pltpu.roll(spread, sh, 1) if sh else spread)[:, edge : edge + block_len] for sh in shifts]
            picked = jnp.where(sub < 4, moved[0], moved[1])
            want = sub % 4 if s == 0 else 3 - sub % 4
            tiles.append(jnp.where(picked == want, 1.0, 0.0))
    hot = jnp.concatenate(tiles, 0).astype(BF16)
    loads[0].wait()
    hot_spec = dot(hot, table[...], ((1,), (0,))).astype(BF16)
    for s in range(2):
        spec_ref[s] = dot(kmer, hot_spec[s * half : (s + 1) * half], ((1,), (0,))).astype(BF16)
    loads[2].wait()
    for t in range(N_TILES):
        w_down = jnp.concatenate(
            [mlp[2 * hidden + h * span + t * group : 2 * hidden + h * span + (t + 1) * group, :] for h in range(hidden // span)], 0
        )
        d_act_ref[t] = dot(w_down, back, ((1,), (0,)))

    for k in range(1, n_seq):
        for n, mask in enumerate(masks):
            piece = gath.at[flip(lane_at, mask), flip(sq, k)]
            sems.arrived(far_base + (k - 1) * len(masks) + n, piece, here)
            to_mate(k, n + 1)
    for k in range(1, n_seq):
        for n in range(len(near)):
            piece = gath.at[flip(lane_at, near[n] + 1), flip(sq, k)]
            sems.arrived(mate_base + (k - 1) * len(near) + n, piece, here)

    for p in range(lanes_in):
        full[:, p * wide : (p + 1) * wide] = gath[p].astype(F32).reshape(channels, wide)
    own = ids[...]
    q_own = table[pl.ds(offset, local_len), :]
    for s in range(2):
        scaled = (full[...] * spec_ref[s].astype(F32)).astype(BF16)
        mine_ids = own if s == 0 else 3 - own
        level = dot(scaled, q_own, ((1,), (1,)))
        residual = jnp.zeros((channels, local_len), F32)
        for a in range(4):
            residual = jnp.where(mine_ids == a, emb_cols[:, a : a + 1], residual)
        level_ref[:, s * local_len : (s + 1) * local_len] = level + residual
    level = level_ref[...]
    mid_scale = lax.rsqrt(jnp.mean(level * level, axis=0, keepdims=True) + 1e-6)
    normed_ref[...] = (level * mid_scale * gain_mid).astype(BF16)
    normed = normed_ref[...]

    order_a = [*range(bits - 1)]
    order_b = [*range(1, bits - 1)] + [0] if bits > 1 else []
    streams = []
    upper = color_rows(chunk)
    split = n_seq // 2

    def bufs_of(index):
        return stage_bufs[index * (bits - 1) : (index + 1) * (bits - 1)]

    for t in range(N_TILES):
        for c, (lo, hi) in enumerate(((0, upper), (upper, chunk))):
            place = lambda q, t=t, lo=lo, hi=hi: sums.at[t, q, pl.ds(lo, hi - lo)]
            streams.append(Stream(sems, order_b if c else order_a, place, bufs_of(2 * t + c)))
    for c, (lo, hi) in enumerate(((0, split), (split, n_seq))):
        place = lambda q, lo=lo, hi=hi: mf.at[q, pl.ds(lo, hi - lo)]
        streams.append(Stream(sems, order_b if c else order_a, place, bufs_of(2 * N_TILES + c)))
    n_first = len(stage_masks(order_a, 0, pairs)) if bits > 1 else 0
    core_base = sems.take(N_TILES)
    zm_base = sems.take(N_TILES * (n_seq - 1))
    cols = channels // n_seq

    def put(t, base, value):
        for h in range(hidden // span):
            start = base + span * h
            i, j = start // part, start % part // span
            grads[t, i % 2, i // 2, j * group : (j + 1) * group, :] = value[h * group : (h + 1) * group, :]

    def swap(t, d_gate, d_up, act):
        for base, left, right in ((0, d_gate, normed), (hidden, d_up, normed), (2 * hidden, act, back)):
            put(t, base, dot(left, right, ((1,), (1,))).astype(BF16))
        sems.start(core_base + t, grads.at[t, 1 - core], recs0.at[t], mate)

    def launch(lead):
        for which in range(n_first):
            for c in (lead, lead + 1):
                streams[c].send_first(dp, sq, which)

    def open_chunk(t):
        sems.arrived(core_base + t, recs0.at[t], here)
        for q in range(pairs):
            sums[t, q] = (grads[t, core, q].astype(F32) + recs0[t, q].astype(F32)).astype(BF16)
        launch(2 * t)

    def take_in(lead, stages):
        for stage in stages:
            for c in (lead, lead + 1):
                streams[c].take_in(stage, dp, sq)

    def across(t):
        total = sums[t, me_q].astype(F32)
        for j in range(n_seq):
            z_out[t, j] = pack(total[:, j * cols : (j + 1) * cols]).astype(BF16)
        for k in range(1, n_seq):
            to = flip(sq, k)
            sems.start(zm_base + t * (n_seq - 1) + k - 1, z_out.at[t, to], z_in.at[t, k - 1], (dp, to))

    def rows_of(base, t):
        return jnp.concatenate(
            [mlp[base + h * span + t * group : base + h * span + (t + 1) * group, :] for h in range(hidden // span)], 0
        )

    for t in range(N_TILES):
        w_gate, w_up, w_down = rows_of(0, t), rows_of(hidden, t), rows_of(2 * hidden, t)
        gate = dot(w_gate, normed, ((1,), (0,)))
        up = dot(w_up, normed, ((1,), (0,)))
        d_act = d_act_ref[t]
        sig = jax.nn.sigmoid(gate)
        silu = gate * sig
        act = (silu * up).astype(BF16)
        d_gate = (d_act * up * (sig + silu * (1.0 - sig))).astype(BF16)
        d_up = (d_act * silu).astype(BF16)
        if t > 0:
            open_chunk(t - 1)
        if t + 1 < N_TILES:
            swap(t, d_gate, d_up, act)
        else:
            keep[0], keep[1], keep[2] = d_gate, d_up, act
        down = dot(w_down, act, ((0,), (0,)))
        down_ref[...] = down if t == 0 else down_ref[...] + down
        d_part = dot(w_gate, d_gate, ((0,), (0,))) + dot(w_up, d_up, ((0,), (0,)))
        d_normed_ref[...] = d_part if t == 0 else d_normed_ref[...] + d_part

    mid_level = level_ref[...]
    unit = mid_level * mid_scale
    d_normed = d_normed_ref[...]
    d_unit = d_normed * gain_mid
    d_level = back.astype(F32) + mid_scale * (d_unit - unit * jnp.mean(d_unit * unit, axis=0, keepdims=True))
    d_bf = d_level.astype(BF16)
    take_in(0, [0])

    grad_filter = jnp.zeros((channels, block_len), F32)
    kmer_sum = jnp.zeros((half, channels), F32)
    for s in range(2):
        d_scaled = dot(d_bf[:, s * local_len : (s + 1) * local_len], q_own, ((1,), (0,)))
        grad_filter = grad_filter + d_scaled * spec_ref[s].astype(F32)
        d_spec = (full[...] * d_scaled).astype(BF16)
        kmer_sum = kmer_sum + dot(hot_spec[s * half : (s + 1) * half], d_spec, ((1,), (1,)))
    grad_filter = grad_filter.astype(BF16)
    groups = n_dp // lanes_in
    piece_rows = own_rows // groups
    for i in range(n_dp):
        block = grad_filter[:, i % lanes_in * wide : (i % lanes_in + 1) * wide]
        for j in range(n_seq):
            top = j * own_rows + i // lanes_in * piece_rows
            gf[i % 2, i // 2, j] = block[top : top + piece_rows, :]
    f_base, s_base = sems.take(), sems.take(bits)
    sems.start(f_base, gf.at[1 - core], rf, mate)
    take_in(2, [0])
    mid_grad = d_normed * unit
    d_low = (d_level - d_bf.astype(F32)).astype(BF16)
    both = jnp.concatenate([own, 3 - own], 1)
    sub8 = lax.broadcasted_iota(jnp.int32, (8, 2 * local_len), 0)
    own_hot = jnp.where(sub8 == both, 1.0, 0.0).astype(BF16)
    ones = jnp.ones((8, 2 * local_len), BF16)
    m_bf = mid_grad.astype(BF16)
    m_low = (mid_grad - m_bf.astype(F32)).astype(BF16)
    base_part_sum = dot(own_hot, d_bf, ((1,), (1,))) + dot(own_hot, d_low, ((1,), (1,)))
    mid_part_sum = dot(ones, m_bf, ((1,), (1,))) + dot(ones, m_low, ((1,), (1,)))
    rows_half = sm.shape[1]
    joined = jnp.concatenate([kmer_sum, base_part_sum, mid_part_sum], 0)
    sm[0] = joined[:rows_half]
    sm[1] = joined[rows_half:]
    sems.start(s_base, sm.at[1 - core], s_rec.at[0], mate)

    sems.arrived(f_base, rf, here)
    for q in range(pairs):
        mf[q] = (gf[core, q].astype(F32) + rf[q].astype(F32)).astype(BF16)
    launch(2 * N_TILES)
    last_t = N_TILES - 1
    swap(last_t, keep[0], keep[1], keep[2])

    def small_step(b):
        sems.arrived(s_base + b, s_rec.at[b], here)
        s_acc[b] = (sm[core] if b == 0 else s_acc[b - 1]) + s_rec[b]
        if b + 1 < bits:
            sems.start(s_base + b + 1, s_acc.at[b], s_rec.at[b + 1], (flip(dp, 2 << b), sq))

    small_step(0)
    take_in(0, range(1, bits - 1))
    across(0)
    open_chunk(last_t)
    take_in(2, range(1, bits - 1))
    across(1)
    combined = (level_ref[...] + down_ref[...]).astype(BF16)
    out[:channels, :] = combined[:, :local_len]
    out[channels:, :] = dot(turn, combined[:, local_len:], ((1,), (0,))).astype(BF16)
    take_in(2 * N_TILES, [0])
    for b in range(1, bits):
        small_step(b)
    take_in(2 * N_TILES, range(1, bits - 1))
    zf_base = sems.take(n_seq - 1)
    for k in range(1, n_seq):
        sems.start(zf_base + k - 1, mf.at[me_q, flip(sq, k)], yf.at[k - 1], (dp, flip(sq, k)))
    zs_base = sems.take(n_seq - 1)
    zs_rec[sq] = s_acc[bits - 1]
    for k in range(1, n_seq):
        sems.start(zs_base + k - 1, s_acc.at[bits - 1], zs_rec.at[sq], (dp, flip(sq, k)))
    take_in(2 * last_t, range(bits - 1))
    across(last_t)

    total = mf[me_q, sq].astype(F32)
    for k in range(1, n_seq):
        sems.arrived(zf_base + k - 1, yf.at[k - 1], here)
        total = total + yf[k - 1].astype(F32)
    filt_out[dp] = total.astype(BF16)
    ring_base = sems.take(n_dp - 1)
    for mask in range(1, n_dp):
        sems.start(ring_base + mask - 1, filt_out.at[dp], filt_out.at[dp], (flip(dp, mask), sq))
    for k in range(1, n_seq):
        sems.arrived(zs_base + k - 1, zs_rec.at[flip(sq, k)], here)
    total = zs_rec[0]
    for j in range(1, n_seq):
        total = total + zs_rec[j]
    small_out[core] = total
    back_base = sems.take()
    sems.start(back_base, small_out.at[core], small_out.at[core], mate)
    for t in range(N_TILES):
        total = z_out[t, sq].astype(F32)
        for k in range(1, n_seq):
            sems.arrived(zm_base + t * (n_seq - 1) + k - 1, z_in.at[t, k - 1], here)
            total = total + z_in[t, k - 1].astype(F32)
        total = unpack(total, chunk, cols)
        for j in range(part // span):
            mlp_out[j * span + t * group : j * span + (t + 1) * group, :] = total[j * group : (j + 1) * group, :]
    sems.arrived(back_base, small_out.at[1 - core], here)
    for mask in range(1, n_dp):
        sems.arrived(ring_base + mask - 1, filt_out.at[flip(dp, mask)], here)
    sems.drain()


def finish_kernel(
    n_taps, layer, mlp_sum, filt, small, embedding, gain_in, taps,
    layer_out, grad_emb, grad_gain, grad_conv, filt_out, grad_mid, mlp_out,
):
    layer_out[...] = layer[...]
    mlp_out[...] = mlp_sum[...]
    n_dp, rows, wide = filt.shape
    lanes_in = filt_out.shape[1] // wide
    for i in range(n_dp):
        top, left = i // lanes_in * rows, i % lanes_in * wide
        filt_out[top : top + rows, left : left + wide] = filt[i].astype(F32)
    channels = embedding.shape[1]
    sums = jnp.concatenate([small[0], small[1]], 0)
    emb = embedding[...]
    gain = gain_in[...].reshape(1, channels)
    base_scale = lax.rsqrt(jnp.mean(emb * emb, axis=1, keepdims=True) + 1e-6)
    unit = emb * base_scale
    base_norm = (unit * gain).astype(BF16).astype(F32)
    d_norm = jnp.zeros(emb.shape, F32)
    for k in range(n_taps):
        part = sums[4 * k : 4 * k + 4, :]
        d_norm = d_norm + part * taps[k : k + 1, :]
        grad_conv[k : k + 1, :] = jnp.sum(part * base_norm, axis=0, keepdims=True)
    grad_gain[...] = jnp.sum(d_norm * unit, axis=0)
    d_unit = d_norm * gain
    base_sum = sums[4 * n_taps : 4 * n_taps + 4, :]
    grad_emb[...] = base_sum + base_scale * (d_unit - unit * jnp.mean(d_unit * unit, axis=1, keepdims=True))
    grad_mid[...] = sums[4 * n_taps + 8 : 4 * n_taps + 9, :].reshape(channels)


def on_device(tokens, embedding, gain_in, conv_taps, long_filter, gain_mid, mlp_weights, cotangent):
    n_dp, n_seq = lax.axis_size("dp"), lax.axis_size("seq")
    own_rows, block_len = long_filter.shape
    channels = own_rows * n_seq
    local_len = tokens.shape[1]
    lanes_in = n_dp
    while block_len % (lanes_in * 128):
        lanes_in //= 2
    wide = block_len // lanes_in
    table = jnp.asarray(dct_table(block_len).T)
    taps = conv_taps.T
    n_taps = taps.shape[0]
    pairs, bits = n_dp // 2, n_dp.bit_length() - 1
    part = mlp_weights.shape[0] // n_dp
    hidden = mlp_weights.shape[0] // 3
    chunk = part // N_TILES
    upper = color_rows(chunk)
    cols = channels // n_seq
    piece = (own_rows // (n_dp // lanes_in), wide)
    rows_half = (4 * n_taps + 16) // 2
    main = pack_rows(chunk, cols)
    packed = (main, 128) if main else (chunk, cols)
    orders = [[*range(bits - 1)], [*range(1, bits - 1)] + [0] if bits > 1 else []]
    two = 2 * local_len

    def v(shape, dtype=BF16):
        return pltpu.VMEM(shape, dtype)

    stage_bufs = []
    for c in range(2 * N_TILES + 2):
        order = orders[c % 2]
        split = n_seq // 2
        if c < 2 * N_TILES:
            tail = (chunk - upper if c % 2 else upper, channels)
        else:
            tail = (n_seq - split if c % 2 else split,) + piece
        for s in range(bits - 1):
            stage_bufs.append(v((len(stage_masks(order, s, pairs)),) + tail))
    n_sems = sem_count(n_dp, n_seq, lanes_in)
    vmem = pl.BlockSpec(memory_space=pltpu.VMEM)
    hbm = pl.BlockSpec(memory_space=pltpu.HBM)
    cot = cotangent[0]
    layer, mlp_sum, filt, small = pl.pallas_call(
        lambda *refs: mega_kernel(n_dp, n_seq, lanes_in, *refs),
        out_shape=(
            jax.ShapeDtypeStruct(cot.shape, BF16),
            jax.ShapeDtypeStruct((part, cols), F32),
            jax.ShapeDtypeStruct((n_dp,) + piece, BF16),
            jax.ShapeDtypeStruct((2, rows_half, channels), F32),
        ),
        in_specs=[vmem] * 6 + [hbm] * 3,
        out_specs=[vmem] * 4,
        scratch_shapes=[
            v(table.shape),
            v(mlp_weights.shape),
            v(cot.shape),
            v((lanes_in, n_seq, own_rows, wide)),
            v((n_seq,) + tokens.shape, jnp.int32),
            v((channels, block_len), F32),
            v((2, channels, block_len)),
            v((channels, two), F32),
            v((channels, two)),
            v((channels, two), F32),
            v((channels, two), F32),
            v((N_TILES, hidden // N_TILES, two), F32),
        ]
        + [
            v((N_TILES, 2, pairs, chunk, channels)),
            v((N_TILES, pairs, chunk, channels)),
            v((N_TILES, pairs, chunk, channels)),
            v((N_TILES, n_seq) + packed),
            v((N_TILES, n_seq - 1) + packed),
            v((3, hidden // N_TILES, two)),
            v((2, pairs, n_seq) + piece),
            v((pairs, n_seq) + piece),
            v((pairs, n_seq) + piece),
            v((n_seq - 1,) + piece),
            v((2, rows_half, channels), F32),
            v((bits, rows_half, channels), F32),
            v((bits, rows_half, channels), F32),
            v((n_seq, rows_half, channels), F32),
        ]
        + stage_bufs
        + [
            pltpu.SemaphoreType.DMA((3,)),
            pltpu.SemaphoreType.DMA((n_sems,)),
            pltpu.SemaphoreType.DMA((n_sems,)),
        ],
        compiler_params=pltpu.CompilerParams(
            collective_id=0, has_side_effects=True, vmem_limit_bytes=62 * 2**20
        ),
        name="mega",
    )(tokens, embedding, gain_in, gain_mid, taps, long_filter, table, mlp_weights, cot)
    layer_out, grad_emb, grad_gain, grad_conv, grad_filter, grad_mid, grad_mlp = pl.pallas_call(
        lambda *refs: finish_kernel(n_taps, *refs),
        out_shape=(
            jax.ShapeDtypeStruct(cot.shape, BF16),
            jax.ShapeDtypeStruct(embedding.shape, F32),
            jax.ShapeDtypeStruct(gain_in.shape, F32),
            jax.ShapeDtypeStruct(taps.shape, F32),
            jax.ShapeDtypeStruct(long_filter.shape, F32),
            jax.ShapeDtypeStruct(gain_mid.shape, F32),
            jax.ShapeDtypeStruct((part, cols), F32),
        ),
        in_specs=[vmem] * 7,
        out_specs=[vmem] * 7,
        compiler_params=pltpu.CompilerParams(vmem_limit_bytes=62 * 2**20),
        name="finish",
    )(layer, mlp_sum, filt, small, embedding, gain_in, taps)
    return layer_out[None], grad_emb, grad_gain, grad_conv.T, grad_filter, grad_mid, grad_mlp


def solution(mesh):
    placed = (P("dp", "seq"), P(), P(), P(), P("seq", None), P(), P(), P("dp", None, "seq"))
    return jax.shard_map(
        on_device,
        mesh=mesh,
        in_specs=placed,
        out_specs=(P("dp", None, "seq"), P(), P(), P(), P("seq", None), P(), P("dp", "seq")),
        check_vma=False,
    )
```

```python
import math

import jax
import jax.numpy as jnp
import numpy as np
from jax import lax
from jax.experimental import pallas as pl
from jax.experimental.pallas import tpu as pltpu
from jax.sharding import PartitionSpec as P

F32 = jnp.float32
BF16 = jnp.bfloat16


def dct_table(length):
    freq = np.arange(length)[:, None]
    place = np.arange(length)[None, :]
    phase = (2 * place + 1) * freq % (4 * length)
    weight = np.where(freq == 0, np.sqrt(1.0 / length), np.sqrt(2.0 / length))
    return (weight * np.cos(np.pi * phase / (2 * length))).astype(np.float32).astype(BF16)


def dot(a, b, dims):
    return lax.dot_general(a, b, (dims, ((), ())), preferred_element_type=F32)


MESH = pl.DeviceIdType.MESH
N_TILES = 3


def flip(index, mask):
    bit = 1
    while bit <= mask:
        if mask & bit:
            index = index + bit * (1 - 2 * lax.rem(index // bit, 2))
        bit *= 2
    return index


def row_group(part, hidden):
    return math.gcd(part, hidden) // N_TILES


def color_rows(rows):
    return rows // 32 * 16 or 8


def pack_rows(rows, cols):
    spare = 128 - cols
    if spare <= 0 or cols % spare or rows % (8 * (cols // spare + 1)):
        return 0
    return rows * cols // 128


def pack(block):
    rows, cols = block.shape
    main = pack_rows(rows, cols)
    if not main:
        return block
    spare = 128 - cols
    rest = jnp.concatenate([block[main:, at : at + spare] for at in range(0, cols, spare)], 0)
    return jnp.concatenate([block[:main], rest], 1)


def unpack(block, rows, cols):
    main = pack_rows(rows, cols)
    if not main:
        return block
    rest = jnp.concatenate([block[at : at + rows - main, cols:] for at in range(0, main, rows - main)], 1)
    return jnp.concatenate([block[:, :cols], rest], 0)


def stage_masks(order, stage, count):
    sent = [
        r
        for r in range(count)
        if (r >> order[stage]) & 1 and not any((r >> o) & 1 for o in order[:stage])
    ]
    return sorted(sent, key=lambda r: [-((r >> o) & 1) for o in order[stage + 1 :]])


class Sems:
    def __init__(self, send, recv):
        self.send, self.recv, self.used, self.started = send, recv, 0, []

    def take(self, count=1):
        first = self.used
        self.used += count
        return first

    def copy(self, index, src, dst, peer):
        return pltpu.make_async_remote_copy(
            src_ref=src,
            dst_ref=dst,
            send_sem=self.send.at[index],
            recv_sem=self.recv.at[index],
            device_id=peer,
            device_id_type=MESH,
        )

    def start(self, index, src, dst, peer):
        copy = self.copy(index, src, dst, peer)
        copy.start()
        self.started.append(copy)

    def arrived(self, index, dst, peer):
        self.copy(index, dst, dst, peer).wait_recv()

    def drain(self):
        for copy in self.started:
            copy.wait_send()


class Stream:
    def __init__(self, sems, order, place, recs):
        self.sems, self.order, self.place, self.recs = sems, order, place, recs
        self.count = 2 ** len(order)
        self.base = [sems.take(len(stage_masks(order, s, self.count))) for s in range(len(order))]

    def send_one(self, stage, mask, dp, sq):
        slot = stage_masks(self.order, stage, self.count).index(mask)
        peer = (flip(dp, 2 << self.order[stage]), sq)
        self.sems.start(
            self.base[stage] + slot, self.place(flip(dp // 2, mask)), self.recs[stage].at[slot], peer
        )

    def send_first(self, dp, sq, which):
        masks = stage_masks(self.order, 0, self.count)
        self.send_one(0, masks[which], dp, sq)

    def take_in(self, stage, dp, sq):
        for slot, mask in enumerate(stage_masks(self.order, stage, self.count)):
            kept = mask ^ (1 << self.order[stage])
            self.sems.arrived(self.base[stage] + slot, self.recs[stage].at[slot], (dp, sq))
            ref = self.place(flip(dp // 2, kept))
            ref[...] = (ref[...].astype(F32) + self.recs[stage][slot].astype(F32)).astype(BF16)
            if stage + 1 < len(self.order) and (kept >> self.order[stage + 1]) & 1:
                self.send_one(stage + 1, kept, dp, sq)


def sem_count(n_dp, n_seq, lanes_in):
    far, pairs = n_seq - 1, n_dp // 2
    bits = n_dp.bit_length() - 1
    return 2 * far + far * lanes_in + N_TILES + 2 + 8 * (pairs - 1) + bits + far + 6 * far + n_dp


def mega_kernel(
    n_dp, n_seq, lanes_in,
    ids_h, emb_h, gin_h, gmid_h, taps_h, shard_h, table_h, mlp_h, cot_h,
    out_h, mlp_out_h, filt_out_h, small_out_h,
    ids, emb, gin, gmid, taps_in, shard, out, mlp_out, filt_out, small_out,
    table, mlp, cot, gath, all_ids, full, spec_ref, level_ref, normed_ref, d_normed_ref, down_ref, d_act_ref,
    grads, recs0, sums, z_out, z_in, keep, gf, rf, mf, yf,
    sm, s_rec, s_acc, zs_rec,
    *rest,
):
    bits = n_dp.bit_length() - 1
    pairs = n_dp // 2
    stage_bufs = list(rest[: 8 * (bits - 1)])
    load_sem, send, recv = rest[8 * (bits - 1) :]
    sems = Sems(send, recv)
    own_rows, block_len = shard.shape
    channels = own_rows * n_seq
    local_len = ids.shape[1]
    hidden = mlp.shape[0] // 3
    n_taps = taps_in.shape[0]
    half = 4 * n_taps
    part = mlp.shape[0] // n_dp
    group = row_group(part, hidden)
    span = N_TILES * group
    chunk = part // N_TILES
    dp, sq = lax.axis_index("dp"), lax.axis_index("seq")
    core = lax.rem(dp, 2)
    me_q = dp // 2
    mate = (flip(dp, 1), sq)
    here = (dp, sq)
    wide = block_len // lanes_in
    lane_at = lax.rem(dp, lanes_in)

    moves = (
        (shard_h, shard), (ids_h, ids), (emb_h, emb), (gin_h, gin), (gmid_h, gmid), (taps_h, taps_in),
        (cot_h, cot), (table_h, table), (mlp_h, mlp),
        (out, out_h), (mlp_out, mlp_out_h), (filt_out, filt_out_h), (small_out, small_out_h),
    )
    loads = [pltpu.make_async_copy(a, b, load_sem.at[n]) for n, (a, b) in enumerate(moves)]
    for load in loads[:9]:
        load.start()
    barrier = pltpu.get_barrier_semaphore()
    for mask in range(1, n_dp):
        pl.semaphore_signal(barrier, inc=1, device_id=(flip(dp, mask), sq), device_id_type=MESH)
    for mask in range(1, n_seq):
        pl.semaphore_signal(barrier, inc=1, device_id=(dp, flip(sq, mask)), device_id_type=MESH)
    loads[0].wait()
    for p in range(lanes_in):
        gath[p, sq] = shard[:, p * wide : (p + 1) * wide].astype(BF16)
    loads[1].wait()
    all_ids[sq] = ids[...]
    pl.semaphore_wait(barrier, n_dp + n_seq - 2)

    id_base = sems.take(n_seq - 1)
    z_base = sems.take(n_seq - 1)
    for k in range(1, n_seq):
        to = (dp, flip(sq, k))
        sems.start(id_base + k - 1, ids, all_ids.at[sq], to)
        sems.start(z_base + k - 1, gath.at[lane_at, sq], gath.at[lane_at, sq], to)

    pad = 128 - 6 - n_taps
    for load in loads[2:6]:
        load.wait()
    rows_all = jnp.concatenate(
        [
            emb[...],
            gin[...].reshape(1, channels),
            gmid[...].reshape(1, channels),
            taps_in[...],
            jnp.zeros((pad, channels), F32),
        ],
        0,
    )
    packed = rows_all.T
    emb_cols, gain_in, gain_mid = packed[:, :4], packed[:, 4:5], packed[:, 5:6]
    taps = packed[:, 6 : 6 + n_taps]
    base_scale = lax.rsqrt(jnp.mean(emb_cols * emb_cols, axis=0, keepdims=True) + 1e-6)
    base_norm = (emb_cols * base_scale * gain_in).astype(BF16).astype(F32)
    lane = lax.broadcasted_iota(jnp.int32, (channels, half), 1)
    tap_part = jnp.zeros((channels, half), F32)
    base_part = jnp.zeros((channels, half), F32)
    for k in range(n_taps):
        tap_part = jnp.where(lane // 4 == k, taps[:, k : k + 1], tap_part)
    for a in range(4):
        base_part = jnp.where(lane % 4 == a, base_norm[:, a : a + 1], base_part)
    kmer = (tap_part * base_part).astype(BF16)
    turn = jnp.where(
        lax.broadcasted_iota(jnp.int32, (channels, channels), 0)
        + lax.broadcasted_iota(jnp.int32, (channels, channels), 1)
        == channels - 1,
        1.0,
        0.0,
    ).astype(BF16)
    loads[6].wait()
    turned = dot(turn, cot[channels:, :], ((1,), (0,))).astype(BF16)
    back = jnp.concatenate([cot[:channels, :], turned], 1)

    masks = [*range(2, lanes_in, 2)]
    near = [0] + masks if lanes_in > 1 else []
    far_base = sems.take((n_seq - 1) * len(masks))
    mate_base = sems.take((n_seq - 1) * len(near))

    def to_mate(k, n):
        piece = gath.at[flip(lane_at, near[n]), flip(sq, k)]
        sems.start(mate_base + (k - 1) * len(near) + n, piece, piece, mate)

    for k in range(1, n_seq):
        piece = gath.at[lane_at, flip(sq, k)]
        sems.arrived(z_base + k - 1, piece, here)
        for n, mask in enumerate(masks):
            sems.start(far_base + (k - 1) * len(masks) + n, piece, piece, (flip(dp, mask), sq))
        if near:
            to_mate(k, 0)
    for k in range(1, n_seq):
        sems.arrived(id_base + k - 1, all_ids.at[flip(sq, k)], here)

    per_block = block_len // local_len
    first = sq // per_block * per_block
    last = first + per_block - 1
    offset = pl.multiple_of((sq - first) * local_len, local_len)
    edge = 128
    before = jnp.where(first > 0, all_ids[jnp.maximum(first - 1, 0)][:, local_len - edge :], 4)
    after = jnp.where(last < n_seq - 1, all_ids[jnp.minimum(last + 1, n_seq - 1)][:, :edge], 4)
    row = jnp.concatenate([before] + [all_ids[first + j] for j in range(per_block)] + [after], 1)
    width = block_len + 2 * edge
    spread = jnp.broadcast_to(row, (8, width))
    sub = lax.broadcasted_iota(jnp.int32, (8, block_len), 0)
    tiles = []
    for s in range(2):
        for k in range(0, n_taps, 2):
            shifts = [(k + i) if s == 0 else (width - k - i) % width for i in range(2)]
            moved = [(pltpu.roll(spread, sh, 1) if sh else spread)[:, edge : edge + block_len] for sh in shifts]
            picked = jnp.where(sub < 4, moved[0], moved[1])
            want = sub % 4 if s == 0 else 3 - sub % 4
            tiles.append(jnp.where(picked == want, 1.0, 0.0))
    hot = jnp.concatenate(tiles, 0).astype(BF16)
    loads[7].wait()
    hot_spec = dot(hot, table[...], ((1,), (0,))).astype(BF16)
    for s in range(2):
        spec_ref[s] = dot(kmer, hot_spec[s * half : (s + 1) * half], ((1,), (0,))).astype(BF16)
    loads[8].wait()
    for t in range(N_TILES):
        w_down = jnp.concatenate(
            [mlp[2 * hidden + h * span + t * group : 2 * hidden + h * span + (t + 1) * group, :] for h in range(hidden // span)], 0
        )
        d_act_ref[t] = dot(w_down, back, ((1,), (0,)))

    for k in range(1, n_seq):
        for n, mask in enumerate(masks):
            piece = gath.at[flip(lane_at, mask), flip(sq, k)]
            sems.arrived(far_base + (k - 1) * len(masks) + n, piece, here)
            to_mate(k, n + 1)
    for k in range(1, n_seq):
        for n in range(len(near)):
            piece = gath.at[flip(lane_at, near[n] + 1), flip(sq, k)]
            sems.arrived(mate_base + (k - 1) * len(near) + n, piece, here)

    for p in range(lanes_in):
        full[:, p * wide : (p + 1) * wide] = gath[p].astype(F32).reshape(channels, wide)
    own = ids[...]
    q_own = table[pl.ds(offset, local_len), :]
    for s in range(2):
        scaled = (full[...] * spec_ref[s].astype(F32)).astype(BF16)
        mine_ids = own if s == 0 else 3 - own
        level = dot(scaled, q_own, ((1,), (1,)))
        residual = jnp.zeros((channels, local_len), F32)
        for a in range(4):
            residual = jnp.where(mine_ids == a, emb_cols[:, a : a + 1], residual)
        level_ref[:, s * local_len : (s + 1) * local_len] = level + residual
    level = level_ref[...]
    mid_scale = lax.rsqrt(jnp.mean(level * level, axis=0, keepdims=True) + 1e-6)
    normed_ref[...] = (level * mid_scale * gain_mid).astype(BF16)
    normed = normed_ref[...]

    order_a = [*range(bits - 1)]
    order_b = [*range(1, bits - 1)] + [0] if bits > 1 else []
    streams = []
    upper = color_rows(chunk)
    split = n_seq // 2

    def bufs_of(index):
        return stage_bufs[index * (bits - 1) : (index + 1) * (bits - 1)]

    for t in range(N_TILES):
        for c, (lo, hi) in enumerate(((0, upper), (upper, chunk))):
            place = lambda q, t=t, lo=lo, hi=hi: sums.at[t, q, pl.ds(lo, hi - lo)]
            streams.append(Stream(sems, order_b if c else order_a, place, bufs_of(2 * t + c)))
    for c, (lo, hi) in enumerate(((0, split), (split, n_seq))):
        place = lambda q, lo=lo, hi=hi: mf.at[q, pl.ds(lo, hi - lo)]
        streams.append(Stream(sems, order_b if c else order_a, place, bufs_of(2 * N_TILES + c)))
    n_first = len(stage_masks(order_a, 0, pairs)) if bits > 1 else 0
    core_base = sems.take(N_TILES)
    zm_base = sems.take(N_TILES * (n_seq - 1))
    cols = channels // n_seq

    def put(t, base, value):
        for h in range(hidden // span):
            start = base + span * h
            i, j = start // part, start % part // span
            grads[t, i % 2, i // 2, j * group : (j + 1) * group, :] = value[h * group : (h + 1) * group, :]

    def swap(t, d_gate, d_up, act):
        for base, left, right in ((0, d_gate, normed), (hidden, d_up, normed), (2 * hidden, act, back)):
            put(t, base, dot(left, right, ((1,), (1,))).astype(BF16))
        sems.start(core_base + t, grads.at[t, 1 - core], recs0.at[t], mate)

    def launch(lead):
        for which in range(n_first):
            for c in (lead, lead + 1):
                streams[c].send_first(dp, sq, which)

    def open_chunk(t):
        sems.arrived(core_base + t, recs0.at[t], here)
        for q in range(pairs):
            sums[t, q] = (grads[t, core, q].astype(F32) + recs0[t, q].astype(F32)).astype(BF16)
        launch(2 * t)

    def take_in(lead, stages):
        for stage in stages:
            for c in (lead, lead + 1):
                streams[c].take_in(stage, dp, sq)

    def across(t):
        total = sums[t, me_q].astype(F32)
        for j in range(n_seq):
            z_out[t, j] = pack(total[:, j * cols : (j + 1) * cols]).astype(BF16)
        for k in range(1, n_seq):
            to = flip(sq, k)
            sems.start(zm_base + t * (n_seq - 1) + k - 1, z_out.at[t, to], z_in.at[t, k - 1], (dp, to))

    def rows_of(base, t):
        return jnp.concatenate(
            [mlp[base + h * span + t * group : base + h * span + (t + 1) * group, :] for h in range(hidden // span)], 0
        )

    for t in range(N_TILES):
        w_gate, w_up, w_down = rows_of(0, t), rows_of(hidden, t), rows_of(2 * hidden, t)
        gate = dot(w_gate, normed, ((1,), (0,)))
        up = dot(w_up, normed, ((1,), (0,)))
        d_act = d_act_ref[t]
        sig = jax.nn.sigmoid(gate)
        silu = gate * sig
        act = (silu * up).astype(BF16)
        d_gate = (d_act * up * (sig + silu * (1.0 - sig))).astype(BF16)
        d_up = (d_act * silu).astype(BF16)
        if t > 0:
            open_chunk(t - 1)
        if t + 1 < N_TILES:
            swap(t, d_gate, d_up, act)
        else:
            keep[0], keep[1], keep[2] = d_gate, d_up, act
        down = dot(w_down, act, ((0,), (0,)))
        down_ref[...] = down if t == 0 else down_ref[...] + down
        d_part = dot(w_gate, d_gate, ((0,), (0,))) + dot(w_up, d_up, ((0,), (0,)))
        d_normed_ref[...] = d_part if t == 0 else d_normed_ref[...] + d_part
    f_base, s_base = sems.take(), sems.take(bits)
    zf_base, zs_base = sems.take(n_seq - 1), sems.take(n_seq - 1)
    ring_base, back_base = sems.take(n_dp - 1), sems.take()
    rows_half = sm.shape[1]
    groups = n_dp // lanes_in
    piece_rows = own_rows // groups
    last_t = N_TILES - 1
    f_at = 2 * N_TILES
    rest_of = range(1, bits - 1)

    def small_step(b):
        sems.arrived(s_base + b, s_rec.at[b], here)
        s_acc[b] = (sm[core] if b == 0 else s_acc[b - 1]) + s_rec[b]
        if b + 1 < bits:
            sems.start(s_base + b + 1, s_acc.at[b], s_rec.at[b + 1], (flip(dp, 2 << b), sq))

    def level_grad():
        unit = level_ref[...] * mid_scale
        d_normed = d_normed_ref[...]
        d_unit = d_normed * gain_mid
        return back.astype(F32) + mid_scale * (d_unit - unit * jnp.mean(d_unit * unit, axis=0, keepdims=True))

    def filter_part(d_bf):
        grad_filter = jnp.zeros((channels, block_len), F32)
        kmer_sum = jnp.zeros((half, channels), F32)
        for s in range(2):
            d_scaled = dot(d_bf[:, s * local_len : (s + 1) * local_len], q_own, ((1,), (0,)))
            grad_filter = grad_filter + d_scaled * spec_ref[s].astype(F32)
            d_spec = (full[...] * d_scaled).astype(BF16)
            kmer_sum = kmer_sum + dot(hot_spec[s * half : (s + 1) * half], d_spec, ((1,), (1,)))
        grad_filter = grad_filter.astype(BF16)
        for i in range(n_dp):
            block = grad_filter[:, i % lanes_in * wide : (i % lanes_in + 1) * wide]
            for j in range(n_seq):
                top = j * own_rows + i // lanes_in * piece_rows
                gf[i % 2, i // 2, j] = block[top : top + piece_rows, :]
        sems.start(f_base, gf.at[1 - core], rf, mate)
        return kmer_sum

    def small_part(d_level, d_bf, kmer_sum):
        mid_grad = d_normed_ref[...] * (level_ref[...] * mid_scale)
        d_low = (d_level - d_bf.astype(F32)).astype(BF16)
        both = jnp.concatenate([own, 3 - own], 1)
        sub8 = lax.broadcasted_iota(jnp.int32, (8, 2 * local_len), 0)
        own_hot = jnp.where(sub8 == both, 1.0, 0.0).astype(BF16)
        ones = jnp.ones((8, 2 * local_len), BF16)
        m_bf = mid_grad.astype(BF16)
        m_low = (mid_grad - m_bf.astype(F32)).astype(BF16)
        base_part_sum = dot(own_hot, d_bf, ((1,), (1,))) + dot(own_hot, d_low, ((1,), (1,)))
        mid_part_sum = dot(ones, m_bf, ((1,), (1,))) + dot(ones, m_low, ((1,), (1,)))
        joined = jnp.concatenate([kmer_sum, base_part_sum, mid_part_sum], 0)
        sm[0] = joined[:rows_half]
        sm[1] = joined[rows_half:]
        sems.start(s_base, sm.at[1 - core], s_rec.at[0], mate)

    def open_filter():
        sems.arrived(f_base, rf, here)
        for q in range(pairs):
            mf[q] = (gf[core, q].astype(F32) + rf[q].astype(F32)).astype(BF16)
        launch(f_at)

    def write_out():
        combined = (level_ref[...] + down_ref[...]).astype(BF16)
        out[:channels, :] = combined[:, :local_len]
        out[channels:, :] = dot(turn, combined[:, local_len:], ((1,), (0,))).astype(BF16)
        loads[9].start()

    def filter_across():
        for k in range(1, n_seq):
            sems.start(zf_base + k - 1, mf.at[me_q, flip(sq, k)], yf.at[k - 1], (dp, flip(sq, k)))

    def small_across():
        zs_rec[sq] = s_acc[bits - 1]
        for k in range(1, n_seq):
            sems.start(zs_base + k - 1, s_acc.at[bits - 1], zs_rec.at[sq], (dp, flip(sq, k)))

    def filter_ring():
        total = mf[me_q, sq].astype(F32)
        for k in range(1, n_seq):
            sems.arrived(zf_base + k - 1, yf.at[k - 1], here)
            total = total + yf[k - 1].astype(F32)
        filt_out[dp] = total.astype(BF16)
        for mask in range(1, n_dp):
            sems.start(ring_base + mask - 1, filt_out.at[dp], filt_out.at[dp], (flip(dp, mask), sq))

    def small_back():
        for k in range(1, n_seq):
            sems.arrived(zs_base + k - 1, zs_rec.at[flip(sq, k)], here)
        total = zs_rec[0]
        for j in range(1, n_seq):
            total = total + zs_rec[j]
        small_out[core] = total
        sems.start(back_base, small_out.at[core], small_out.at[core], mate)

    def finish_chunk(t):
        total = z_out[t, sq].astype(F32)
        for k in range(1, n_seq):
            sems.arrived(zm_base + t * (n_seq - 1) + k - 1, z_in.at[t, k - 1], here)
            total = total + z_in[t, k - 1].astype(F32)
        total = unpack(total, chunk, cols)
        for j in range(part // span):
            mlp_out[j * span + t * group : j * span + (t + 1) * group, :] = total[j * group : (j + 1) * group, :]

    d_level = level_grad()
    d_bf = d_level.astype(BF16)
    kmer_sum = filter_part(d_bf)
    small_part(d_level, d_bf, kmer_sum)
    take_in(0, [0])
    open_filter()
    swap(last_t, keep[0], keep[1], keep[2])
    take_in(2, [0])
    small_step(0)
    take_in(0, rest_of)
    across(0)
    take_in(f_at, [0])
    open_chunk(last_t)
    small_step(1)
    write_out()
    take_in(f_at, rest_of)
    filter_across()
    take_in(2, rest_of)
    across(1)
    for b in range(2, bits):
        small_step(b)
    small_across()
    take_in(2 * last_t, [0])
    take_in(2 * last_t, rest_of)
    across(last_t)
    filter_ring()
    small_back()
    finish_chunk(0)
    finish_chunk(1)
    finish_chunk(last_t)
    loads[10].start()
    sems.arrived(back_base, small_out.at[1 - core], here)
    loads[12].start()
    for mask in range(1, n_dp):
        sems.arrived(ring_base + mask - 1, filt_out.at[flip(dp, mask)], here)
    loads[11].start()
    sems.drain()
    for load in loads[9:]:
        load.wait()


def finish_kernel(
    n_taps, layer_h, mlp_sum_h, filt_h, small_h, emb_h, gain_h, taps_h,
    layer_out_h, grad_emb_h, grad_gain_h, grad_conv_h, filt_out_h, grad_mid_h, mlp_out_h,
    layer, mlp_sum, filt, small, embedding, gain_in, taps,
    grad_emb, grad_gain, grad_conv, filt_out, grad_mid, sem,
):
    moves = (
        (layer_h, layer), (filt_h, filt), (small_h, small), (emb_h, embedding), (gain_h, gain_in), (taps_h, taps),
        (mlp_sum_h, mlp_sum), (layer, layer_out_h), (mlp_sum, mlp_out_h), (filt_out, filt_out_h),
        (grad_emb, grad_emb_h), (grad_gain, grad_gain_h), (grad_conv, grad_conv_h), (grad_mid, grad_mid_h),
    )
    copies = [pltpu.make_async_copy(a, b, sem.at[n]) for n, (a, b) in enumerate(moves)]
    for copy in copies[:7]:
        copy.start()
    copies[0].wait()
    copies[7].start()
    copies[1].wait()
    n_dp, rows, wide = filt.shape
    lanes_in = filt_out.shape[1] // wide
    for i in range(n_dp):
        top, left = i // lanes_in * rows, i % lanes_in * wide
        filt_out[top : top + rows, left : left + wide] = filt[i].astype(F32)
    copies[9].start()
    for copy in copies[2:7]:
        copy.wait()
    copies[8].start()
    channels = embedding.shape[1]
    sums = jnp.concatenate([small[0], small[1]], 0)
    emb = embedding[...]
    gain = gain_in[...].reshape(1, channels)
    base_scale = lax.rsqrt(jnp.mean(emb * emb, axis=1, keepdims=True) + 1e-6)
    unit = emb * base_scale
    base_norm = (unit * gain).astype(BF16).astype(F32)
    d_norm = jnp.zeros(emb.shape, F32)
    for k in range(n_taps):
        part = sums[4 * k : 4 * k + 4, :]
        d_norm = d_norm + part * taps[k : k + 1, :]
        grad_conv[k : k + 1, :] = jnp.sum(part * base_norm, axis=0, keepdims=True)
    grad_gain[...] = jnp.sum(d_norm * unit, axis=0)
    d_unit = d_norm * gain
    base_sum = sums[4 * n_taps : 4 * n_taps + 4, :]
    grad_emb[...] = base_sum + base_scale * (d_unit - unit * jnp.mean(d_unit * unit, axis=1, keepdims=True))
    grad_mid[...] = sums[4 * n_taps + 8 : 4 * n_taps + 9, :].reshape(channels)
    for copy in copies[10:]:
        copy.start()
    for copy in copies[7:]:
        copy.wait()


def on_device(tokens, embedding, gain_in, conv_taps, long_filter, gain_mid, mlp_weights, cotangent):
    n_dp, n_seq = lax.axis_size("dp"), lax.axis_size("seq")
    own_rows, block_len = long_filter.shape
    channels = own_rows * n_seq
    local_len = tokens.shape[1]
    lanes_in = n_dp
    while block_len % (lanes_in * 128):
        lanes_in //= 2
    wide = block_len // lanes_in
    table = jnp.asarray(dct_table(block_len).T)
    taps = conv_taps.T
    n_taps = taps.shape[0]
    pairs, bits = n_dp // 2, n_dp.bit_length() - 1
    part = mlp_weights.shape[0] // n_dp
    hidden = mlp_weights.shape[0] // 3
    chunk = part // N_TILES
    upper = color_rows(chunk)
    cols = channels // n_seq
    piece = (own_rows // (n_dp // lanes_in), wide)
    rows_half = (4 * n_taps + 16) // 2
    main = pack_rows(chunk, cols)
    packed = (main, 128) if main else (chunk, cols)
    orders = [[*range(bits - 1)], [*range(1, bits - 1)] + [0] if bits > 1 else []]
    two = 2 * local_len

    def v(shape, dtype=BF16):
        return pltpu.VMEM(shape, dtype)

    stage_bufs = []
    for c in range(2 * N_TILES + 2):
        order = orders[c % 2]
        split = n_seq // 2
        if c < 2 * N_TILES:
            tail = (chunk - upper if c % 2 else upper, channels)
        else:
            tail = (n_seq - split if c % 2 else split,) + piece
        for s in range(bits - 1):
            stage_bufs.append(v((len(stage_masks(order, s, pairs)),) + tail))
    n_sems = sem_count(n_dp, n_seq, lanes_in)
    vmem = pl.BlockSpec(memory_space=pltpu.VMEM)
    hbm = pl.BlockSpec(memory_space=pltpu.HBM)
    cot = cotangent[0]
    layer, mlp_sum, filt, small = pl.pallas_call(
        lambda *refs: mega_kernel(n_dp, n_seq, lanes_in, *refs),
        out_shape=(
            jax.ShapeDtypeStruct(cot.shape, BF16),
            jax.ShapeDtypeStruct((part, cols), F32),
            jax.ShapeDtypeStruct((n_dp,) + piece, BF16),
            jax.ShapeDtypeStruct((2, rows_half, channels), F32),
        ),
        in_specs=[hbm] * 9,
        out_specs=[hbm] * 4,
        scratch_shapes=[
            v(tokens.shape, jnp.int32),
            v(embedding.shape, F32),
            v(gain_in.shape, F32),
            v(gain_mid.shape, F32),
            v(taps.shape, F32),
            v(long_filter.shape, F32),
            v(cot.shape),
            v((part, cols), F32),
            v((n_dp,) + piece),
            v((2, rows_half, channels), F32),
            v(table.shape),
            v(mlp_weights.shape),
            v(cot.shape),
            v((lanes_in, n_seq, own_rows, wide)),
            v((n_seq,) + tokens.shape, jnp.int32),
            v((channels, block_len), F32),
            v((2, channels, block_len)),
            v((channels, two), F32),
            v((channels, two)),
            v((channels, two), F32),
            v((channels, two), F32),
            v((N_TILES, hidden // N_TILES, two), F32),
        ]
        + [
            v((N_TILES, 2, pairs, chunk, channels)),
            v((N_TILES, pairs, chunk, channels)),
            v((N_TILES, pairs, chunk, channels)),
            v((N_TILES, n_seq) + packed),
            v((N_TILES, n_seq - 1) + packed),
            v((3, hidden // N_TILES, two)),
            v((2, pairs, n_seq) + piece),
            v((pairs, n_seq) + piece),
            v((pairs, n_seq) + piece),
            v((n_seq - 1,) + piece),
            v((2, rows_half, channels), F32),
            v((bits, rows_half, channels), F32),
            v((bits, rows_half, channels), F32),
            v((n_seq, rows_half, channels), F32),
        ]
        + stage_bufs
        + [
            pltpu.SemaphoreType.DMA((13,)),
            pltpu.SemaphoreType.DMA((n_sems,)),
            pltpu.SemaphoreType.DMA((n_sems,)),
        ],
        compiler_params=pltpu.CompilerParams(
            collective_id=0, has_side_effects=True, vmem_limit_bytes=62 * 2**20
        ),
        name="mega",
    )(tokens, embedding, gain_in, gain_mid, taps, long_filter, table, mlp_weights, cot)
    layer_out, grad_emb, grad_gain, grad_conv, grad_filter, grad_mid, grad_mlp = pl.pallas_call(
        lambda *refs: finish_kernel(n_taps, *refs),
        out_shape=(
            jax.ShapeDtypeStruct(cot.shape, BF16),
            jax.ShapeDtypeStruct(embedding.shape, F32),
            jax.ShapeDtypeStruct(gain_in.shape, F32),
            jax.ShapeDtypeStruct(taps.shape, F32),
            jax.ShapeDtypeStruct(long_filter.shape, F32),
            jax.ShapeDtypeStruct(gain_mid.shape, F32),
            jax.ShapeDtypeStruct((part, cols), F32),
        ),
        in_specs=[hbm] * 7,
        out_specs=[hbm] * 7,
        scratch_shapes=[
            v(cot.shape),
            v((part, cols), F32),
            v((n_dp,) + piece),
            v((2, rows_half, channels), F32),
            v(embedding.shape, F32),
            v(gain_in.shape, F32),
            v(taps.shape, F32),
            v(embedding.shape, F32),
            v(gain_in.shape, F32),
            v(taps.shape, F32),
            v(long_filter.shape, F32),
            v(gain_mid.shape, F32),
            pltpu.SemaphoreType.DMA((14,)),
        ],
        compiler_params=pltpu.CompilerParams(vmem_limit_bytes=62 * 2**20),
        name="finish",
    )(layer, mlp_sum, filt, small, embedding, gain_in, taps)
    return layer_out[None], grad_emb, grad_gain, grad_conv.T, grad_filter, grad_mid, grad_mlp


def solution(mesh):
    placed = (P("dp", "seq"), P(), P(), P(), P("seq", None), P(), P(), P("dp", None, "seq"))
    return jax.shard_map(
        on_device,
        mesh=mesh,
        in_specs=placed,
        out_specs=(P("dp", None, "seq"), P(), P(), P(), P("seq", None), P(), P("dp", "seq")),
        check_vma=False,
    )
```

```python
import math

import jax
import jax.numpy as jnp
import numpy as np
from jax import lax
from jax.experimental import pallas as pl
from jax.experimental.pallas import tpu as pltpu
from jax.sharding import PartitionSpec as P

F32 = jnp.float32
BF16 = jnp.bfloat16


def dct_table(length):
    freq = np.arange(length)[:, None]
    place = np.arange(length)[None, :]
    phase = (2 * place + 1) * freq % (4 * length)
    weight = np.where(freq == 0, np.sqrt(1.0 / length), np.sqrt(2.0 / length))
    return (weight * np.cos(np.pi * phase / (2 * length))).astype(np.float32).astype(BF16)


def dot(a, b, dims):
    return lax.dot_general(a, b, (dims, ((), ())), preferred_element_type=F32)


MESH = pl.DeviceIdType.MESH
N_TILES = 3


def flip(index, mask):
    bit = 1
    while bit <= mask:
        if mask & bit:
            index = index + bit * (1 - 2 * lax.rem(index // bit, 2))
        bit *= 2
    return index


def row_group(part, hidden):
    return math.gcd(part, hidden) // N_TILES


def color_rows(rows):
    return rows // 32 * 16 or 8


def pack_rows(rows, cols):
    spare = 128 - cols
    if spare <= 0 or cols % spare or rows % (8 * (cols // spare + 1)):
        return 0
    return rows * cols // 128


def pack(block):
    rows, cols = block.shape
    main = pack_rows(rows, cols)
    if not main:
        return block
    spare = 128 - cols
    rest = jnp.concatenate([block[main:, at : at + spare] for at in range(0, cols, spare)], 0)
    return jnp.concatenate([block[:main], rest], 1)


def unpack(block, rows, cols):
    main = pack_rows(rows, cols)
    if not main:
        return block
    rest = jnp.concatenate([block[at : at + rows - main, cols:] for at in range(0, main, rows - main)], 1)
    return jnp.concatenate([block[:, :cols], rest], 0)


def stage_masks(order, stage, count):
    sent = [
        r
        for r in range(count)
        if (r >> order[stage]) & 1 and not any((r >> o) & 1 for o in order[:stage])
    ]
    return sorted(sent, key=lambda r: [-((r >> o) & 1) for o in order[stage + 1 :]])


class Sems:
    def __init__(self, send, recv):
        self.send, self.recv, self.used, self.started = send, recv, 0, []

    def take(self, count=1):
        first = self.used
        self.used += count
        return first

    def copy(self, index, src, dst, peer):
        return pltpu.make_async_remote_copy(
            src_ref=src,
            dst_ref=dst,
            send_sem=self.send.at[index],
            recv_sem=self.recv.at[index],
            device_id=peer,
            device_id_type=MESH,
        )

    def start(self, index, src, dst, peer):
        copy = self.copy(index, src, dst, peer)
        copy.start()
        self.started.append(copy)

    def arrived(self, index, dst, peer):
        self.copy(index, dst, dst, peer).wait_recv()

    def drain(self):
        for copy in self.started:
            copy.wait_send()


class Stream:
    def __init__(self, sems, order, place, recs):
        self.sems, self.order, self.place, self.recs = sems, order, place, recs
        self.count = 2 ** len(order)
        self.base = [sems.take(len(stage_masks(order, s, self.count))) for s in range(len(order))]

    def send_one(self, stage, mask, dp, sq):
        slot = stage_masks(self.order, stage, self.count).index(mask)
        peer = (flip(dp, 2 << self.order[stage]), sq)
        self.sems.start(
            self.base[stage] + slot, self.place(flip(dp // 2, mask)), self.recs[stage].at[slot], peer
        )

    def send_first(self, dp, sq, which):
        masks = stage_masks(self.order, 0, self.count)
        self.send_one(0, masks[which], dp, sq)

    def take_in(self, stage, dp, sq):
        for slot, mask in enumerate(stage_masks(self.order, stage, self.count)):
            kept = mask ^ (1 << self.order[stage])
            self.sems.arrived(self.base[stage] + slot, self.recs[stage].at[slot], (dp, sq))
            ref = self.place(flip(dp // 2, kept))
            ref[...] = (ref[...].astype(F32) + self.recs[stage][slot].astype(F32)).astype(BF16)
            if stage + 1 < len(self.order) and (kept >> self.order[stage + 1]) & 1:
                self.send_one(stage + 1, kept, dp, sq)


def sem_count(n_dp, n_seq, lanes_in):
    far, pairs = n_seq - 1, n_dp // 2
    bits = n_dp.bit_length() - 1
    return 2 * far + far * lanes_in + N_TILES + 2 + 8 * (pairs - 1) + bits + far + 6 * far + n_dp


def mega_kernel(
    n_dp, n_seq, lanes_in,
    ids_h, emb_h, gin_h, gmid_h, taps_h, shard_h, table_h, mlp_h, cot_h,
    out, mlp_out, filt_out, small_out,
    ids, emb, gin, gmid, taps_in, shard,
    table, mlp, cot, gath, all_ids, full, spec_ref, level_ref, normed_ref, d_normed_ref, down_ref, d_act_ref,
    grads, recs0, sums, z_out, z_in, keep, gf, rf, mf, yf,
    sm, s_rec, s_acc, zs_rec,
    *rest,
):
    bits = n_dp.bit_length() - 1
    pairs = n_dp // 2
    stage_bufs = list(rest[: 8 * (bits - 1)])
    load_sem, send, recv = rest[8 * (bits - 1) :]
    sems = Sems(send, recv)
    own_rows, block_len = shard.shape
    channels = own_rows * n_seq
    local_len = ids.shape[1]
    hidden = mlp.shape[0] // 3
    n_taps = taps_in.shape[0]
    half = 4 * n_taps
    part = mlp.shape[0] // n_dp
    group = row_group(part, hidden)
    span = N_TILES * group
    chunk = part // N_TILES
    dp, sq = lax.axis_index("dp"), lax.axis_index("seq")
    core = lax.rem(dp, 2)
    me_q = dp // 2
    mate = (flip(dp, 1), sq)
    here = (dp, sq)
    wide = block_len // lanes_in
    lane_at = lax.rem(dp, lanes_in)

    moves = (
        (shard_h, shard), (ids_h, ids), (emb_h, emb), (gin_h, gin), (gmid_h, gmid), (taps_h, taps_in),
        (cot_h, cot), (table_h, table), (mlp_h, mlp),
    )
    loads = [pltpu.make_async_copy(a, b, load_sem.at[n]) for n, (a, b) in enumerate(moves)]
    for load in loads:
        load.start()
    barrier = pltpu.get_barrier_semaphore()
    for mask in range(1, n_dp):
        pl.semaphore_signal(barrier, inc=1, device_id=(flip(dp, mask), sq), device_id_type=MESH)
    for mask in range(1, n_seq):
        pl.semaphore_signal(barrier, inc=1, device_id=(dp, flip(sq, mask)), device_id_type=MESH)
    loads[0].wait()
    for p in range(lanes_in):
        gath[p, sq] = shard[:, p * wide : (p + 1) * wide].astype(BF16)
    loads[1].wait()
    all_ids[sq] = ids[...]
    pl.semaphore_wait(barrier, n_dp + n_seq - 2)

    id_base = sems.take(n_seq - 1)
    z_base = sems.take(n_seq - 1)
    for k in range(1, n_seq):
        to = (dp, flip(sq, k))
        sems.start(id_base + k - 1, ids, all_ids.at[sq], to)
        sems.start(z_base + k - 1, gath.at[lane_at, sq], gath.at[lane_at, sq], to)

    pad = 128 - 6 - n_taps
    for load in loads[2:6]:
        load.wait()
    rows_all = jnp.concatenate(
        [
            emb[...],
            gin[...].reshape(1, channels),
            gmid[...].reshape(1, channels),
            taps_in[...],
            jnp.zeros((pad, channels), F32),
        ],
        0,
    )
    packed = rows_all.T
    emb_cols, gain_in, gain_mid = packed[:, :4], packed[:, 4:5], packed[:, 5:6]
    taps = packed[:, 6 : 6 + n_taps]
    base_scale = lax.rsqrt(jnp.mean(emb_cols * emb_cols, axis=0, keepdims=True) + 1e-6)
    base_norm = (emb_cols * base_scale * gain_in).astype(BF16).astype(F32)
    lane = lax.broadcasted_iota(jnp.int32, (channels, half), 1)
    tap_part = jnp.zeros((channels, half), F32)
    base_part = jnp.zeros((channels, half), F32)
    for k in range(n_taps):
        tap_part = jnp.where(lane // 4 == k, taps[:, k : k + 1], tap_part)
    for a in range(4):
        base_part = jnp.where(lane % 4 == a, base_norm[:, a : a + 1], base_part)
    kmer = (tap_part * base_part).astype(BF16)
    turn = jnp.where(
        lax.broadcasted_iota(jnp.int32, (channels, channels), 0)
        + lax.broadcasted_iota(jnp.int32, (channels, channels), 1)
        == channels - 1,
        1.0,
        0.0,
    ).astype(BF16)
    loads[6].wait()
    turned = dot(turn, cot[channels:, :], ((1,), (0,))).astype(BF16)
    back = jnp.concatenate([cot[:channels, :], turned], 1)

    masks = [*range(2, lanes_in, 2)]
    near = [0] + masks if lanes_in > 1 else []
    far_base = sems.take((n_seq - 1) * len(masks))
    mate_base = sems.take((n_seq - 1) * len(near))

    def to_mate(k, n):
        piece = gath.at[flip(lane_at, near[n]), flip(sq, k)]
        sems.start(mate_base + (k - 1) * len(near) + n, piece, piece, mate)

    for k in range(1, n_seq):
        piece = gath.at[lane_at, flip(sq, k)]
        sems.arrived(z_base + k - 1, piece, here)
        for n, mask in enumerate(masks):
            sems.start(far_base + (k - 1) * len(masks) + n, piece, piece, (flip(dp, mask), sq))
        if near:
            to_mate(k, 0)
    for k in range(1, n_seq):
        sems.arrived(id_base + k - 1, all_ids.at[flip(sq, k)], here)

    per_block = block_len // local_len
    first = sq // per_block * per_block
    last = first + per_block - 1
    offset = pl.multiple_of((sq - first) * local_len, local_len)
    edge = 128
    before = jnp.where(first > 0, all_ids[jnp.maximum(first - 1, 0)][:, local_len - edge :], 4)
    after = jnp.where(last < n_seq - 1, all_ids[jnp.minimum(last + 1, n_seq - 1)][:, :edge], 4)
    row = jnp.concatenate([before] + [all_ids[first + j] for j in range(per_block)] + [after], 1)
    width = block_len + 2 * edge
    spread = jnp.broadcast_to(row, (8, width))
    sub = lax.broadcasted_iota(jnp.int32, (8, block_len), 0)
    tiles = []
    for s in range(2):
        for k in range(0, n_taps, 2):
            shifts = [(k + i) if s == 0 else (width - k - i) % width for i in range(2)]
            moved = [(pltpu.roll(spread, sh, 1) if sh else spread)[:, edge : edge + block_len] for sh in shifts]
            picked = jnp.where(sub < 4, moved[0], moved[1])
            want = sub % 4 if s == 0 else 3 - sub % 4
            tiles.append(jnp.where(picked == want, 1.0, 0.0))
    hot = jnp.concatenate(tiles, 0).astype(BF16)
    loads[7].wait()
    hot_spec = dot(hot, table[...], ((1,), (0,))).astype(BF16)
    for s in range(2):
        spec_ref[s] = dot(kmer, hot_spec[s * half : (s + 1) * half], ((1,), (0,))).astype(BF16)
    loads[8].wait()
    for t in range(N_TILES):
        w_down = jnp.concatenate(
            [mlp[2 * hidden + h * span + t * group : 2 * hidden + h * span + (t + 1) * group, :] for h in range(hidden // span)], 0
        )
        d_act_ref[t] = dot(w_down, back, ((1,), (0,)))

    for k in range(1, n_seq):
        for n, mask in enumerate(masks):
            piece = gath.at[flip(lane_at, mask), flip(sq, k)]
            sems.arrived(far_base + (k - 1) * len(masks) + n, piece, here)
            to_mate(k, n + 1)
    for k in range(1, n_seq):
        for n in range(len(near)):
            piece = gath.at[flip(lane_at, near[n] + 1), flip(sq, k)]
            sems.arrived(mate_base + (k - 1) * len(near) + n, piece, here)

    for p in range(lanes_in):
        full[:, p * wide : (p + 1) * wide] = gath[p].astype(F32).reshape(channels, wide)
    own = ids[...]
    q_own = table[pl.ds(offset, local_len), :]
    for s in range(2):
        scaled = (full[...] * spec_ref[s].astype(F32)).astype(BF16)
        mine_ids = own if s == 0 else 3 - own
        level = dot(scaled, q_own, ((1,), (1,)))
        residual = jnp.zeros((channels, local_len), F32)
        for a in range(4):
            residual = jnp.where(mine_ids == a, emb_cols[:, a : a + 1], residual)
        level_ref[:, s * local_len : (s + 1) * local_len] = level + residual
    level = level_ref[...]
    mid_scale = lax.rsqrt(jnp.mean(level * level, axis=0, keepdims=True) + 1e-6)
    normed_ref[...] = (level * mid_scale * gain_mid).astype(BF16)
    normed = normed_ref[...]

    order_a = [*range(bits - 1)]
    order_b = [*range(1, bits - 1)] + [0] if bits > 1 else []
    streams = []
    upper = color_rows(chunk)
    split = n_seq // 2

    def bufs_of(index):
        return stage_bufs[index * (bits - 1) : (index + 1) * (bits - 1)]

    for t in range(N_TILES):
        for c, (lo, hi) in enumerate(((0, upper), (upper, chunk))):
            place = lambda q, t=t, lo=lo, hi=hi: sums.at[t, q, pl.ds(lo, hi - lo)]
            streams.append(Stream(sems, order_b if c else order_a, place, bufs_of(2 * t + c)))
    for c, (lo, hi) in enumerate(((0, split), (split, n_seq))):
        place = lambda q, lo=lo, hi=hi: mf.at[q, pl.ds(lo, hi - lo)]
        streams.append(Stream(sems, order_b if c else order_a, place, bufs_of(2 * N_TILES + c)))
    n_first = len(stage_masks(order_a, 0, pairs)) if bits > 1 else 0
    core_base = sems.take(N_TILES)
    zm_base = sems.take(N_TILES * (n_seq - 1))
    cols = channels // n_seq

    def put(t, base, value):
        for h in range(hidden // span):
            start = base + span * h
            i, j = start // part, start % part // span
            grads[t, i % 2, i // 2, j * group : (j + 1) * group, :] = value[h * group : (h + 1) * group, :]

    def swap(t, d_gate, d_up, act):
        for base, left, right in ((0, d_gate, normed), (hidden, d_up, normed), (2 * hidden, act, back)):
            put(t, base, dot(left, right, ((1,), (1,))).astype(BF16))
        sems.start(core_base + t, grads.at[t, 1 - core], recs0.at[t], mate)

    def launch(lead):
        for which in range(n_first):
            for c in (lead, lead + 1):
                streams[c].send_first(dp, sq, which)

    def open_chunk(t):
        sems.arrived(core_base + t, recs0.at[t], here)
        for q in range(pairs):
            sums[t, q] = (grads[t, core, q].astype(F32) + recs0[t, q].astype(F32)).astype(BF16)
        launch(2 * t)

    def take_in(lead, stages):
        for stage in stages:
            for c in (lead, lead + 1):
                streams[c].take_in(stage, dp, sq)

    def across(t):
        total = sums[t, me_q].astype(F32)
        for j in range(n_seq):
            z_out[t, j] = pack(total[:, j * cols : (j + 1) * cols]).astype(BF16)
        for k in range(1, n_seq):
            to = flip(sq, k)
            sems.start(zm_base + t * (n_seq - 1) + k - 1, z_out.at[t, to], z_in.at[t, k - 1], (dp, to))

    def rows_of(base, t):
        return jnp.concatenate(
            [mlp[base + h * span + t * group : base + h * span + (t + 1) * group, :] for h in range(hidden // span)], 0
        )

    for t in range(N_TILES):
        w_gate, w_up, w_down = rows_of(0, t), rows_of(hidden, t), rows_of(2 * hidden, t)
        gate = dot(w_gate, normed, ((1,), (0,)))
        up = dot(w_up, normed, ((1,), (0,)))
        d_act = d_act_ref[t]
        sig = jax.nn.sigmoid(gate)
        silu = gate * sig
        act = (silu * up).astype(BF16)
        d_gate = (d_act * up * (sig + silu * (1.0 - sig))).astype(BF16)
        d_up = (d_act * silu).astype(BF16)
        if t > 0:
            open_chunk(t - 1)
        if t + 1 < N_TILES:
            swap(t, d_gate, d_up, act)
        else:
            keep[0], keep[1], keep[2] = d_gate, d_up, act
        down = dot(w_down, act, ((0,), (0,)))
        down_ref[...] = down if t == 0 else down_ref[...] + down
        d_part = dot(w_gate, d_gate, ((0,), (0,))) + dot(w_up, d_up, ((0,), (0,)))
        d_normed_ref[...] = d_part if t == 0 else d_normed_ref[...] + d_part
    f_base, s_base = sems.take(), sems.take(bits)
    zf_base, zs_base = sems.take(n_seq - 1), sems.take(n_seq - 1)
    ring_base, back_base = sems.take(n_dp - 1), sems.take()
    rows_half = sm.shape[1]
    groups = n_dp // lanes_in
    piece_rows = own_rows // groups
    last_t = N_TILES - 1
    f_at = 2 * N_TILES
    rest_of = range(1, bits - 1)

    def small_step(b):
        sems.arrived(s_base + b, s_rec.at[b], here)
        s_acc[b] = (sm[core] if b == 0 else s_acc[b - 1]) + s_rec[b]
        if b + 1 < bits:
            sems.start(s_base + b + 1, s_acc.at[b], s_rec.at[b + 1], (flip(dp, 2 << b), sq))

    def level_grad():
        unit = level_ref[...] * mid_scale
        d_normed = d_normed_ref[...]
        d_unit = d_normed * gain_mid
        return back.astype(F32) + mid_scale * (d_unit - unit * jnp.mean(d_unit * unit, axis=0, keepdims=True))

    def filter_part(d_bf):
        grad_filter = jnp.zeros((channels, block_len), F32)
        kmer_sum = jnp.zeros((half, channels), F32)
        for s in range(2):
            d_scaled = dot(d_bf[:, s * local_len : (s + 1) * local_len], q_own, ((1,), (0,)))
            grad_filter = grad_filter + d_scaled * spec_ref[s].astype(F32)
            d_spec = (full[...] * d_scaled).astype(BF16)
            kmer_sum = kmer_sum + dot(hot_spec[s * half : (s + 1) * half], d_spec, ((1,), (1,)))
        grad_filter = grad_filter.astype(BF16)
        for i in range(n_dp):
            block = grad_filter[:, i % lanes_in * wide : (i % lanes_in + 1) * wide]
            for j in range(n_seq):
                top = j * own_rows + i // lanes_in * piece_rows
                gf[i % 2, i // 2, j] = block[top : top + piece_rows, :]
        sems.start(f_base, gf.at[1 - core], rf, mate)
        return kmer_sum

    def small_part(d_level, d_bf, kmer_sum):
        mid_grad = d_normed_ref[...] * (level_ref[...] * mid_scale)
        d_low = (d_level - d_bf.astype(F32)).astype(BF16)
        both = jnp.concatenate([own, 3 - own], 1)
        sub8 = lax.broadcasted_iota(jnp.int32, (8, 2 * local_len), 0)
        own_hot = jnp.where(sub8 == both, 1.0, 0.0).astype(BF16)
        ones = jnp.ones((8, 2 * local_len), BF16)
        m_bf = mid_grad.astype(BF16)
        m_low = (mid_grad - m_bf.astype(F32)).astype(BF16)
        base_part_sum = dot(own_hot, d_bf, ((1,), (1,))) + dot(own_hot, d_low, ((1,), (1,)))
        mid_part_sum = dot(ones, m_bf, ((1,), (1,))) + dot(ones, m_low, ((1,), (1,)))
        joined = jnp.concatenate([kmer_sum, base_part_sum, mid_part_sum], 0)
        sm[0] = joined[:rows_half]
        sm[1] = joined[rows_half:]
        sems.start(s_base, sm.at[1 - core], s_rec.at[0], mate)

    def open_filter():
        sems.arrived(f_base, rf, here)
        for q in range(pairs):
            mf[q] = (gf[core, q].astype(F32) + rf[q].astype(F32)).astype(BF16)
        launch(f_at)

    def write_out():
        combined = (level_ref[...] + down_ref[...]).astype(BF16)
        out[:channels, :] = combined[:, :local_len]
        out[channels:, :] = dot(turn, combined[:, local_len:], ((1,), (0,))).astype(BF16)

    def filter_across():
        for k in range(1, n_seq):
            sems.start(zf_base + k - 1, mf.at[me_q, flip(sq, k)], yf.at[k - 1], (dp, flip(sq, k)))

    def small_across():
        zs_rec[sq] = s_acc[bits - 1]
        for k in range(1, n_seq):
            sems.start(zs_base + k - 1, s_acc.at[bits - 1], zs_rec.at[sq], (dp, flip(sq, k)))

    def filter_ring():
        total = mf[me_q, sq].astype(F32)
        for k in range(1, n_seq):
            sems.arrived(zf_base + k - 1, yf.at[k - 1], here)
            total = total + yf[k - 1].astype(F32)
        filt_out[dp] = total.astype(BF16)
        for mask in range(1, n_dp):
            sems.start(ring_base + mask - 1, filt_out.at[dp], filt_out.at[dp], (flip(dp, mask), sq))

    def small_back():
        for k in range(1, n_seq):
            sems.arrived(zs_base + k - 1, zs_rec.at[flip(sq, k)], here)
        total = zs_rec[0]
        for j in range(1, n_seq):
            total = total + zs_rec[j]
        small_out[core] = total
        sems.start(back_base, small_out.at[core], small_out.at[core], mate)

    def finish_chunk(t):
        total = z_out[t, sq].astype(F32)
        for k in range(1, n_seq):
            sems.arrived(zm_base + t * (n_seq - 1) + k - 1, z_in.at[t, k - 1], here)
            total = total + z_in[t, k - 1].astype(F32)
        total = unpack(total, chunk, cols)
        for j in range(part // span):
            mlp_out[j * span + t * group : j * span + (t + 1) * group, :] = total[j * group : (j + 1) * group, :]

    d_level = level_grad()
    d_bf = d_level.astype(BF16)
    kmer_sum = filter_part(d_bf)
    small_part(d_level, d_bf, kmer_sum)
    take_in(0, [0])
    open_filter()
    swap(last_t, keep[0], keep[1], keep[2])
    take_in(2, [0])
    small_step(0)
    take_in(0, rest_of)
    across(0)
    take_in(f_at, [0])
    open_chunk(last_t)
    small_step(1)
    write_out()
    take_in(f_at, rest_of)
    filter_across()
    take_in(2, rest_of)
    across(1)
    for b in range(2, bits):
        small_step(b)
    small_across()
    take_in(2 * last_t, [0])
    take_in(2 * last_t, rest_of)
    across(last_t)
    filter_ring()
    small_back()
    finish_chunk(0)
    finish_chunk(1)
    finish_chunk(last_t)
    sems.arrived(back_base, small_out.at[1 - core], here)
    for mask in range(1, n_dp):
        sems.arrived(ring_base + mask - 1, filt_out.at[flip(dp, mask)], here)
    sems.drain()


def finish_kernel(
    n_taps, layer, mlp_sum, filt, small, embedding, gain_in, taps,
    layer_out_h, grad_emb_h, grad_gain_h, grad_conv_h, filt_out_h, grad_mid_h, mlp_out_h,
    grad_emb, grad_gain, grad_conv, filt_out, grad_mid, sem,
):
    moves = (
        (layer, layer_out_h), (mlp_sum, mlp_out_h), (filt_out, filt_out_h),
        (grad_emb, grad_emb_h), (grad_gain, grad_gain_h), (grad_conv, grad_conv_h), (grad_mid, grad_mid_h),
    )
    copies = [pltpu.make_async_copy(a, b, sem.at[n]) for n, (a, b) in enumerate(moves)]
    copies[0].start()
    copies[1].start()
    n_dp, rows, wide = filt.shape
    lanes_in = filt_out.shape[1] // wide
    for i in range(n_dp):
        top, left = i // lanes_in * rows, i % lanes_in * wide
        filt_out[top : top + rows, left : left + wide] = filt[i].astype(F32)
    copies[2].start()
    channels = embedding.shape[1]
    sums = jnp.concatenate([small[0], small[1]], 0)
    emb = embedding[...]
    gain = gain_in[...].reshape(1, channels)
    base_scale = lax.rsqrt(jnp.mean(emb * emb, axis=1, keepdims=True) + 1e-6)
    unit = emb * base_scale
    base_norm = (unit * gain).astype(BF16).astype(F32)
    d_norm = jnp.zeros(emb.shape, F32)
    for k in range(n_taps):
        part = sums[4 * k : 4 * k + 4, :]
        d_norm = d_norm + part * taps[k : k + 1, :]
        grad_conv[k : k + 1, :] = jnp.sum(part * base_norm, axis=0, keepdims=True)
    grad_gain[...] = jnp.sum(d_norm * unit, axis=0)
    d_unit = d_norm * gain
    base_sum = sums[4 * n_taps : 4 * n_taps + 4, :]
    grad_emb[...] = base_sum + base_scale * (d_unit - unit * jnp.mean(d_unit * unit, axis=1, keepdims=True))
    grad_mid[...] = sums[4 * n_taps + 8 : 4 * n_taps + 9, :].reshape(channels)
    for copy in copies[3:]:
        copy.start()
    for copy in copies:
        copy.wait()


def on_device(tokens, embedding, gain_in, conv_taps, long_filter, gain_mid, mlp_weights, cotangent):
    n_dp, n_seq = lax.axis_size("dp"), lax.axis_size("seq")
    own_rows, block_len = long_filter.shape
    channels = own_rows * n_seq
    local_len = tokens.shape[1]
    lanes_in = n_dp
    while block_len % (lanes_in * 128):
        lanes_in //= 2
    wide = block_len // lanes_in
    table = jnp.asarray(dct_table(block_len).T)
    taps = conv_taps.T
    n_taps = taps.shape[0]
    pairs, bits = n_dp // 2, n_dp.bit_length() - 1
    part = mlp_weights.shape[0] // n_dp
    hidden = mlp_weights.shape[0] // 3
    chunk = part // N_TILES
    upper = color_rows(chunk)
    cols = channels // n_seq
    piece = (own_rows // (n_dp // lanes_in), wide)
    rows_half = (4 * n_taps + 16) // 2
    main = pack_rows(chunk, cols)
    packed = (main, 128) if main else (chunk, cols)
    orders = [[*range(bits - 1)], [*range(1, bits - 1)] + [0] if bits > 1 else []]
    two = 2 * local_len

    def v(shape, dtype=BF16):
        return pltpu.VMEM(shape, dtype)

    stage_bufs = []
    for c in range(2 * N_TILES + 2):
        order = orders[c % 2]
        split = n_seq // 2
        if c < 2 * N_TILES:
            tail = (chunk - upper if c % 2 else upper, channels)
        else:
            tail = (n_seq - split if c % 2 else split,) + piece
        for s in range(bits - 1):
            stage_bufs.append(v((len(stage_masks(order, s, pairs)),) + tail))
    n_sems = sem_count(n_dp, n_seq, lanes_in)
    vmem = pl.BlockSpec(memory_space=pltpu.VMEM)
    hbm = pl.BlockSpec(memory_space=pltpu.HBM)
    cot = cotangent[0]
    operands = [tokens, embedding, gain_in, gain_mid, taps, long_filter, table, mlp_weights, cot]
    operands = [pltpu.with_memory_space_constraint(x, pltpu.HBM) for x in operands]
    layer, mlp_sum, filt, small = pl.pallas_call(
        lambda *refs: mega_kernel(n_dp, n_seq, lanes_in, *refs),
        out_shape=(
            jax.ShapeDtypeStruct(cot.shape, BF16),
            jax.ShapeDtypeStruct((part, cols), F32),
            jax.ShapeDtypeStruct((n_dp,) + piece, BF16),
            jax.ShapeDtypeStruct((2, rows_half, channels), F32),
        ),
        in_specs=[hbm] * 9,
        out_specs=[vmem] * 4,
        scratch_shapes=[
            v(tokens.shape, jnp.int32),
            v(embedding.shape, F32),
            v(gain_in.shape, F32),
            v(gain_mid.shape, F32),
            v(taps.shape, F32),
            v(long_filter.shape, F32),
            v(table.shape),
            v(mlp_weights.shape),
            v(cot.shape),
            v((lanes_in, n_seq, own_rows, wide)),
            v((n_seq,) + tokens.shape, jnp.int32),
            v((channels, block_len), F32),
            v((2, channels, block_len)),
            v((channels, two), F32),
            v((channels, two)),
            v((channels, two), F32),
            v((channels, two), F32),
            v((N_TILES, hidden // N_TILES, two), F32),
        ]
        + [
            v((N_TILES, 2, pairs, chunk, channels)),
            v((N_TILES, pairs, chunk, channels)),
            v((N_TILES, pairs, chunk, channels)),
            v((N_TILES, n_seq) + packed),
            v((N_TILES, n_seq - 1) + packed),
            v((3, hidden // N_TILES, two)),
            v((2, pairs, n_seq) + piece),
            v((pairs, n_seq) + piece),
            v((pairs, n_seq) + piece),
            v((n_seq - 1,) + piece),
            v((2, rows_half, channels), F32),
            v((bits, rows_half, channels), F32),
            v((bits, rows_half, channels), F32),
            v((n_seq, rows_half, channels), F32),
        ]
        + stage_bufs
        + [
            pltpu.SemaphoreType.DMA((9,)),
            pltpu.SemaphoreType.DMA((n_sems,)),
            pltpu.SemaphoreType.DMA((n_sems,)),
        ],
        compiler_params=pltpu.CompilerParams(
            collective_id=0, has_side_effects=True, vmem_limit_bytes=34 * 2**20
        ),
        name="mega",
    )(*operands)
    layer_out, grad_emb, grad_gain, grad_conv, grad_filter, grad_mid, grad_mlp = pl.pallas_call(
        lambda *refs: finish_kernel(n_taps, *refs),
        out_shape=(
            jax.ShapeDtypeStruct(cot.shape, BF16),
            jax.ShapeDtypeStruct(embedding.shape, F32),
            jax.ShapeDtypeStruct(gain_in.shape, F32),
            jax.ShapeDtypeStruct(taps.shape, F32),
            jax.ShapeDtypeStruct(long_filter.shape, F32),
            jax.ShapeDtypeStruct(gain_mid.shape, F32),
            jax.ShapeDtypeStruct((part, cols), F32),
        ),
        in_specs=[vmem] * 7,
        out_specs=[hbm] * 7,
        scratch_shapes=[
            v(embedding.shape, F32),
            v(gain_in.shape, F32),
            v(taps.shape, F32),
            v(long_filter.shape, F32),
            v(gain_mid.shape, F32),
            pltpu.SemaphoreType.DMA((7,)),
        ],
        compiler_params=pltpu.CompilerParams(vmem_limit_bytes=8 * 2**20),
        name="finish",
    )(layer, mlp_sum, filt, small, embedding, gain_in, taps)
    return layer_out[None], grad_emb, grad_gain, grad_conv.T, grad_filter, grad_mid, grad_mlp


def solution(mesh):
    placed = (P("dp", "seq"), P(), P(), P(), P("seq", None), P(), P(), P("dp", None, "seq"))
    return jax.shard_map(
        on_device,
        mesh=mesh,
        in_specs=placed,
        out_specs=(P("dp", None, "seq"), P(), P(), P(), P("seq", None), P(), P("dp", "seq")),
        check_vma=False,
    )
```

```python
import math

import jax
import jax.numpy as jnp
import numpy as np
from jax import lax
from jax.experimental import pallas as pl
from jax.experimental.pallas import tpu as pltpu
from jax.sharding import PartitionSpec as P

F32 = jnp.float32
BF16 = jnp.bfloat16


def dct_table(length):
    freq = np.arange(length)[:, None]
    place = np.arange(length)[None, :]
    phase = (2 * place + 1) * freq % (4 * length)
    weight = np.where(freq == 0, np.sqrt(1.0 / length), np.sqrt(2.0 / length))
    return (weight * np.cos(np.pi * phase / (2 * length))).astype(np.float32).astype(BF16)


def dot(a, b, dims):
    return lax.dot_general(a, b, (dims, ((), ())), preferred_element_type=F32)


MESH = pl.DeviceIdType.MESH
N_TILES = 3


def flip(index, mask):
    bit = 1
    while bit <= mask:
        if mask & bit:
            index = index + bit * (1 - 2 * lax.rem(index // bit, 2))
        bit *= 2
    return index


def row_group(part, hidden):
    return math.gcd(part, hidden) // N_TILES


def color_rows(rows):
    return rows // 32 * 16 or 8


def pack_rows(rows, cols):
    spare = 128 - cols
    if spare <= 0 or cols % spare or rows % (8 * (cols // spare + 1)):
        return 0
    return rows * cols // 128


def pack(block):
    rows, cols = block.shape
    main = pack_rows(rows, cols)
    if not main:
        return block
    spare = 128 - cols
    rest = jnp.concatenate([block[main:, at : at + spare] for at in range(0, cols, spare)], 0)
    return jnp.concatenate([block[:main], rest], 1)


def unpack(block, rows, cols):
    main = pack_rows(rows, cols)
    if not main:
        return block
    rest = jnp.concatenate([block[at : at + rows - main, cols:] for at in range(0, main, rows - main)], 1)
    return jnp.concatenate([block[:, :cols], rest], 0)


def stage_masks(order, stage, count):
    sent = [
        r
        for r in range(count)
        if (r >> order[stage]) & 1 and not any((r >> o) & 1 for o in order[:stage])
    ]
    return sorted(sent, key=lambda r: [-((r >> o) & 1) for o in order[stage + 1 :]])


class Sems:
    def __init__(self, send, recv):
        self.send, self.recv, self.used, self.started = send, recv, 0, []

    def take(self, count=1):
        first = self.used
        self.used += count
        return first

    def copy(self, index, src, dst, peer):
        return pltpu.make_async_remote_copy(
            src_ref=src,
            dst_ref=dst,
            send_sem=self.send.at[index],
            recv_sem=self.recv.at[index],
            device_id=peer,
            device_id_type=MESH,
        )

    def start(self, index, src, dst, peer):
        copy = self.copy(index, src, dst, peer)
        copy.start()
        self.started.append(copy)

    def arrived(self, index, dst, peer):
        self.copy(index, dst, dst, peer).wait_recv()

    def drain(self):
        for copy in self.started:
            copy.wait_send()


class Stream:
    def __init__(self, sems, order, place, recs):
        self.sems, self.order, self.place, self.recs = sems, order, place, recs
        self.count = 2 ** len(order)
        self.base = [sems.take(len(stage_masks(order, s, self.count))) for s in range(len(order))]

    def send_one(self, stage, mask, dp, sq):
        slot = stage_masks(self.order, stage, self.count).index(mask)
        peer = (flip(dp, 2 << self.order[stage]), sq)
        self.sems.start(
            self.base[stage] + slot, self.place(flip(dp // 2, mask)), self.recs[stage].at[slot], peer
        )

    def send_first(self, dp, sq, which):
        masks = stage_masks(self.order, 0, self.count)
        self.send_one(0, masks[which], dp, sq)

    def take_in(self, stage, dp, sq):
        for slot, mask in enumerate(stage_masks(self.order, stage, self.count)):
            kept = mask ^ (1 << self.order[stage])
            self.sems.arrived(self.base[stage] + slot, self.recs[stage].at[slot], (dp, sq))
            ref = self.place(flip(dp // 2, kept))
            ref[...] = (ref[...].astype(F32) + self.recs[stage][slot].astype(F32)).astype(BF16)
            if stage + 1 < len(self.order) and (kept >> self.order[stage + 1]) & 1:
                self.send_one(stage + 1, kept, dp, sq)


def sem_count(n_dp, n_seq, lanes_in):
    far, pairs = n_seq - 1, n_dp // 2
    bits = n_dp.bit_length() - 1
    return 2 * far + far * lanes_in + N_TILES + 2 + 8 * (pairs - 1) + bits + far + 6 * far + n_dp


def mega_kernel(
    n_dp, n_seq, lanes_in,
    ids_h, emb_h, gin_h, gmid_h, taps_h, shard_h, table_h, mlp_h, cot_h,
    out, mlp_out, filt_out, small_out,
    ids, emb, gin, gmid, taps_in, shard,
    table, mlp, cot, gath, all_ids, full, spec_ref, level_ref, normed_ref, d_normed_ref, down_ref, d_act_ref,
    grads, recs0, sums, z_out, z_in, keep, gf, rf, mf, yf,
    sm, s_rec, s_acc, zs_rec,
    *rest,
):
    bits = n_dp.bit_length() - 1
    pairs = n_dp // 2
    stage_bufs = list(rest[: 8 * (bits - 1)])
    load_sem, send, recv = rest[8 * (bits - 1) :]
    sems = Sems(send, recv)
    own_rows, block_len = shard.shape
    channels = own_rows * n_seq
    local_len = ids.shape[1]
    hidden = mlp.shape[0] // 3
    n_taps = taps_in.shape[0]
    half = 4 * n_taps
    part = mlp.shape[0] // n_dp
    group = row_group(part, hidden)
    span = N_TILES * group
    chunk = part // N_TILES
    dp, sq = lax.axis_index("dp"), lax.axis_index("seq")
    core = lax.rem(dp, 2)
    me_q = dp // 2
    mate = (flip(dp, 1), sq)
    here = (dp, sq)
    wide = block_len // lanes_in
    lane_at = lax.rem(dp, lanes_in)

    moves = (
        (shard_h, shard), (ids_h, ids), (emb_h, emb), (gin_h, gin), (gmid_h, gmid), (taps_h, taps_in),
        (cot_h, cot), (table_h, table), (mlp_h, mlp),
    )
    loads = [pltpu.make_async_copy(a, b, load_sem.at[n]) for n, (a, b) in enumerate(moves)]
    for load in loads:
        load.start()
    barrier = pltpu.get_barrier_semaphore()
    for mask in range(1, n_dp):
        pl.semaphore_signal(barrier, inc=1, device_id=(flip(dp, mask), sq), device_id_type=MESH)
    for mask in range(1, n_seq):
        pl.semaphore_signal(barrier, inc=1, device_id=(dp, flip(sq, mask)), device_id_type=MESH)
    loads[0].wait()
    gath[lane_at, sq] = shard[:, pl.ds(pl.multiple_of(lane_at * wide, wide), wide)].astype(BF16)
    loads[1].wait()
    all_ids[sq] = ids[...]
    pl.semaphore_wait(barrier, n_dp + n_seq - 2)

    id_base = sems.take(n_seq - 1)
    z_base = sems.take(n_seq - 1)
    for k in range(1, n_seq):
        to = (dp, flip(sq, k))
        sems.start(id_base + k - 1, ids, all_ids.at[sq], to)
        sems.start(z_base + k - 1, gath.at[lane_at, sq], gath.at[lane_at, sq], to)

    pad = 128 - 6 - n_taps
    for load in loads[2:6]:
        load.wait()
    rows_all = jnp.concatenate(
        [
            emb[...],
            gin[...].reshape(1, channels),
            gmid[...].reshape(1, channels),
            taps_in[...],
            jnp.zeros((pad, channels), F32),
        ],
        0,
    )
    packed = rows_all.T
    emb_cols, gain_in, gain_mid = packed[:, :4], packed[:, 4:5], packed[:, 5:6]
    taps = packed[:, 6 : 6 + n_taps]
    base_scale = lax.rsqrt(jnp.mean(emb_cols * emb_cols, axis=0, keepdims=True) + 1e-6)
    base_norm = (emb_cols * base_scale * gain_in).astype(BF16).astype(F32)
    lane = lax.broadcasted_iota(jnp.int32, (channels, half), 1)
    tap_part = jnp.zeros((channels, half), F32)
    base_part = jnp.zeros((channels, half), F32)
    for k in range(n_taps):
        tap_part = jnp.where(lane // 4 == k, taps[:, k : k + 1], tap_part)
    for a in range(4):
        base_part = jnp.where(lane % 4 == a, base_norm[:, a : a + 1], base_part)
    kmer = (tap_part * base_part).astype(BF16)
    turn = jnp.where(
        lax.broadcasted_iota(jnp.int32, (channels, channels), 0)
        + lax.broadcasted_iota(jnp.int32, (channels, channels), 1)
        == channels - 1,
        1.0,
        0.0,
    ).astype(BF16)
    loads[6].wait()
    turned = dot(turn, cot[channels:, :], ((1,), (0,))).astype(BF16)
    back = jnp.concatenate([cot[:channels, :], turned], 1)

    for p in range(1, lanes_in):
        at = flip(lane_at, p)
        gath[at, sq] = shard[:, pl.ds(pl.multiple_of(at * wide, wide), wide)].astype(BF16)
    masks = [*range(2, lanes_in, 2)]
    near = [0] + masks if lanes_in > 1 else []
    far_base = sems.take((n_seq - 1) * len(masks))
    mate_base = sems.take((n_seq - 1) * len(near))

    def to_mate(k, n):
        piece = gath.at[flip(lane_at, near[n]), flip(sq, k)]
        sems.start(mate_base + (k - 1) * len(near) + n, piece, piece, mate)

    for k in range(1, n_seq):
        piece = gath.at[lane_at, flip(sq, k)]
        sems.arrived(z_base + k - 1, piece, here)
        for n, mask in enumerate(masks):
            sems.start(far_base + (k - 1) * len(masks) + n, piece, piece, (flip(dp, mask), sq))
        if near:
            to_mate(k, 0)
    for k in range(1, n_seq):
        sems.arrived(id_base + k - 1, all_ids.at[flip(sq, k)], here)

    per_block = block_len // local_len
    first = sq // per_block * per_block
    last = first + per_block - 1
    offset = pl.multiple_of((sq - first) * local_len, local_len)
    edge = 128
    before = jnp.where(first > 0, all_ids[jnp.maximum(first - 1, 0)][:, local_len - edge :], 4)
    after = jnp.where(last < n_seq - 1, all_ids[jnp.minimum(last + 1, n_seq - 1)][:, :edge], 4)
    row = jnp.concatenate([before] + [all_ids[first + j] for j in range(per_block)] + [after], 1)
    width = block_len + 2 * edge
    spread = jnp.broadcast_to(row, (8, width))
    sub = lax.broadcasted_iota(jnp.int32, (8, block_len), 0)
    tiles = []
    for s in range(2):
        for k in range(0, n_taps, 2):
            shifts = [(k + i) if s == 0 else (width - k - i) % width for i in range(2)]
            moved = [(pltpu.roll(spread, sh, 1) if sh else spread)[:, edge : edge + block_len] for sh in shifts]
            picked = jnp.where(sub < 4, moved[0], moved[1])
            want = sub % 4 if s == 0 else 3 - sub % 4
            tiles.append(jnp.where(picked == want, 1.0, 0.0))
    hot = jnp.concatenate(tiles, 0).astype(BF16)
    loads[7].wait()
    hot_spec = dot(hot, table[...], ((1,), (0,))).astype(BF16)
    for s in range(2):
        spec_ref[s] = dot(kmer, hot_spec[s * half : (s + 1) * half], ((1,), (0,))).astype(BF16)
    loads[8].wait()
    for t in range(N_TILES):
        w_down = jnp.concatenate(
            [mlp[2 * hidden + h * span + t * group : 2 * hidden + h * span + (t + 1) * group, :] for h in range(hidden // span)], 0
        )
        d_act_ref[t] = dot(w_down, back, ((1,), (0,)))

    for k in range(1, n_seq):
        for n, mask in enumerate(masks):
            piece = gath.at[flip(lane_at, mask), flip(sq, k)]
            sems.arrived(far_base + (k - 1) * len(masks) + n, piece, here)
            to_mate(k, n + 1)
    for k in range(1, n_seq):
        for n in range(len(near)):
            piece = gath.at[flip(lane_at, near[n] + 1), flip(sq, k)]
            sems.arrived(mate_base + (k - 1) * len(near) + n, piece, here)

    for p in range(lanes_in):
        full[:, p * wide : (p + 1) * wide] = gath[p].astype(F32).reshape(channels, wide)
    own = ids[...]
    q_own = table[pl.ds(offset, local_len), :]
    for s in range(2):
        scaled = (full[...] * spec_ref[s].astype(F32)).astype(BF16)
        mine_ids = own if s == 0 else 3 - own
        level = dot(scaled, q_own, ((1,), (1,)))
        residual = jnp.zeros((channels, local_len), F32)
        for a in range(4):
            residual = jnp.where(mine_ids == a, emb_cols[:, a : a + 1], residual)
        level_ref[:, s * local_len : (s + 1) * local_len] = level + residual
    level = level_ref[...]
    mid_scale = lax.rsqrt(jnp.mean(level * level, axis=0, keepdims=True) + 1e-6)
    normed_ref[...] = (level * mid_scale * gain_mid).astype(BF16)
    normed = normed_ref[...]

    order_a = [*range(bits - 1)]
    order_b = [*range(1, bits - 1)] + [0] if bits > 1 else []
    streams = []
    upper = color_rows(chunk)
    split = n_seq // 2

    def bufs_of(index):
        return stage_bufs[index * (bits - 1) : (index + 1) * (bits - 1)]

    for t in range(N_TILES):
        for c, (lo, hi) in enumerate(((0, upper), (upper, chunk))):
            place = lambda q, t=t, lo=lo, hi=hi: sums.at[t, q, pl.ds(lo, hi - lo)]
            streams.append(Stream(sems, order_b if c else order_a, place, bufs_of(2 * t + c)))
    for c, (lo, hi) in enumerate(((0, split), (split, n_seq))):
        place = lambda q, lo=lo, hi=hi: mf.at[q, pl.ds(lo, hi - lo)]
        streams.append(Stream(sems, order_b if c else order_a, place, bufs_of(2 * N_TILES + c)))
    n_first = len(stage_masks(order_a, 0, pairs)) if bits > 1 else 0
    core_base = sems.take(N_TILES)
    zm_base = sems.take(N_TILES * (n_seq - 1))
    cols = channels // n_seq

    def put(t, base, value):
        for h in range(hidden // span):
            start = base + span * h
            i, j = start // part, start % part // span
            grads[t, i % 2, i // 2, j * group : (j + 1) * group, :] = value[h * group : (h + 1) * group, :]

    def swap(t, d_gate, d_up, act):
        for base, left, right in ((0, d_gate, normed), (hidden, d_up, normed), (2 * hidden, act, back)):
            put(t, base, dot(left, right, ((1,), (1,))).astype(BF16))
        sems.start(core_base + t, grads.at[t, 1 - core], recs0.at[t], mate)

    def launch(lead):
        for which in range(n_first):
            for c in (lead, lead + 1):
                streams[c].send_first(dp, sq, which)

    def open_chunk(t):
        sems.arrived(core_base + t, recs0.at[t], here)
        for q in range(pairs):
            sums[t, q] = (grads[t, core, q].astype(F32) + recs0[t, q].astype(F32)).astype(BF16)
        launch(2 * t)

    def take_in(lead, stages):
        for stage in stages:
            for c in (lead, lead + 1):
                streams[c].take_in(stage, dp, sq)

    def across(t):
        total = sums[t, me_q].astype(F32)
        for j in range(n_seq):
            z_out[t, j] = pack(total[:, j * cols : (j + 1) * cols]).astype(BF16)
        for k in range(1, n_seq):
            to = flip(sq, k)
            sems.start(zm_base + t * (n_seq - 1) + k - 1, z_out.at[t, to], z_in.at[t, k - 1], (dp, to))

    def rows_of(base, t):
        return jnp.concatenate(
            [mlp[base + h * span + t * group : base + h * span + (t + 1) * group, :] for h in range(hidden // span)], 0
        )

    for t in range(N_TILES):
        w_gate, w_up, w_down = rows_of(0, t), rows_of(hidden, t), rows_of(2 * hidden, t)
        gate = dot(w_gate, normed, ((1,), (0,)))
        up = dot(w_up, normed, ((1,), (0,)))
        d_act = d_act_ref[t]
        sig = jax.nn.sigmoid(gate)
        silu = gate * sig
        act = (silu * up).astype(BF16)
        d_gate = (d_act * up * (sig + silu * (1.0 - sig))).astype(BF16)
        d_up = (d_act * silu).astype(BF16)
        if t > 0:
            open_chunk(t - 1)
        if t + 1 < N_TILES:
            swap(t, d_gate, d_up, act)
        else:
            keep[0], keep[1], keep[2] = d_gate, d_up, act
        down = dot(w_down, act, ((0,), (0,)))
        down_ref[...] = down if t == 0 else down_ref[...] + down
        d_part = dot(w_gate, d_gate, ((0,), (0,))) + dot(w_up, d_up, ((0,), (0,)))
        d_normed_ref[...] = d_part if t == 0 else d_normed_ref[...] + d_part
    f_base, s_base = sems.take(), sems.take(bits)
    zf_base, zs_base = sems.take(n_seq - 1), sems.take(n_seq - 1)
    ring_base, back_base = sems.take(n_dp - 1), sems.take()
    rows_half = sm.shape[1]
    groups = n_dp // lanes_in
    piece_rows = own_rows // groups
    last_t = N_TILES - 1
    f_at = 2 * N_TILES
    rest_of = range(1, bits - 1)

    def small_step(b):
        sems.arrived(s_base + b, s_rec.at[b], here)
        s_acc[b] = (sm[core] if b == 0 else s_acc[b - 1]) + s_rec[b]
        if b + 1 < bits:
            sems.start(s_base + b + 1, s_acc.at[b], s_rec.at[b + 1], (flip(dp, 2 << b), sq))

    def level_grad():
        unit = level_ref[...] * mid_scale
        d_normed = d_normed_ref[...]
        d_unit = d_normed * gain_mid
        return back.astype(F32) + mid_scale * (d_unit - unit * jnp.mean(d_unit * unit, axis=0, keepdims=True))

    def filter_part(d_bf):
        grad_filter = jnp.zeros((channels, block_len), F32)
        kmer_sum = jnp.zeros((half, channels), F32)
        for s in range(2):
            d_scaled = dot(d_bf[:, s * local_len : (s + 1) * local_len], q_own, ((1,), (0,)))
            grad_filter = grad_filter + d_scaled * spec_ref[s].astype(F32)
            d_spec = (full[...] * d_scaled).astype(BF16)
            kmer_sum = kmer_sum + dot(hot_spec[s * half : (s + 1) * half], d_spec, ((1,), (1,)))
        grad_filter = grad_filter.astype(BF16)
        for i in range(n_dp):
            block = grad_filter[:, i % lanes_in * wide : (i % lanes_in + 1) * wide]
            for j in range(n_seq):
                top = j * own_rows + i // lanes_in * piece_rows
                gf[i % 2, i // 2, j] = block[top : top + piece_rows, :]
        sems.start(f_base, gf.at[1 - core], rf, mate)
        return kmer_sum

    def small_part(d_level, d_bf, kmer_sum):
        mid_grad = d_normed_ref[...] * (level_ref[...] * mid_scale)
        d_low = (d_level - d_bf.astype(F32)).astype(BF16)
        both = jnp.concatenate([own, 3 - own], 1)
        sub8 = lax.broadcasted_iota(jnp.int32, (8, 2 * local_len), 0)
        own_hot = jnp.where(sub8 == both, 1.0, 0.0).astype(BF16)
        ones = jnp.ones((8, 2 * local_len), BF16)
        m_bf = mid_grad.astype(BF16)
        m_low = (mid_grad - m_bf.astype(F32)).astype(BF16)
        base_part_sum = dot(own_hot, d_bf, ((1,), (1,))) + dot(own_hot, d_low, ((1,), (1,)))
        mid_part_sum = dot(ones, m_bf, ((1,), (1,))) + dot(ones, m_low, ((1,), (1,)))
        joined = jnp.concatenate([kmer_sum, base_part_sum, mid_part_sum], 0)
        sm[0] = joined[:rows_half]
        sm[1] = joined[rows_half:]
        sems.start(s_base, sm.at[1 - core], s_rec.at[0], mate)

    def open_filter():
        sems.arrived(f_base, rf, here)
        for q in range(pairs):
            mf[q] = (gf[core, q].astype(F32) + rf[q].astype(F32)).astype(BF16)
        launch(f_at)

    def write_out():
        combined = (level_ref[...] + down_ref[...]).astype(BF16)
        out[:channels, :] = combined[:, :local_len]
        out[channels:, :] = dot(turn, combined[:, local_len:], ((1,), (0,))).astype(BF16)

    def filter_across():
        for k in range(1, n_seq):
            sems.start(zf_base + k - 1, mf.at[me_q, flip(sq, k)], yf.at[k - 1], (dp, flip(sq, k)))

    def small_across():
        zs_rec[sq] = s_acc[bits - 1]
        for k in range(1, n_seq):
            sems.start(zs_base + k - 1, s_acc.at[bits - 1], zs_rec.at[sq], (dp, flip(sq, k)))

    def filter_ring():
        total = mf[me_q, sq].astype(F32)
        for k in range(1, n_seq):
            sems.arrived(zf_base + k - 1, yf.at[k - 1], here)
            total = total + yf[k - 1].astype(F32)
        filt_out[dp] = total.astype(BF16)
        for mask in range(1, n_dp):
            sems.start(ring_base + mask - 1, filt_out.at[dp], filt_out.at[dp], (flip(dp, mask), sq))

    def small_back():
        for k in range(1, n_seq):
            sems.arrived(zs_base + k - 1, zs_rec.at[flip(sq, k)], here)
        total = zs_rec[0]
        for j in range(1, n_seq):
            total = total + zs_rec[j]
        small_out[core] = total
        sems.start(back_base, small_out.at[core], small_out.at[core], mate)

    def finish_chunk(t):
        total = z_out[t, sq].astype(F32)
        for k in range(1, n_seq):
            sems.arrived(zm_base + t * (n_seq - 1) + k - 1, z_in.at[t, k - 1], here)
            total = total + z_in[t, k - 1].astype(F32)
        total = unpack(total, chunk, cols)
        for j in range(part // span):
            mlp_out[j * span + t * group : j * span + (t + 1) * group, :] = total[j * group : (j + 1) * group, :]

    d_level = level_grad()
    d_bf = d_level.astype(BF16)
    kmer_sum = filter_part(d_bf)
    small_part(d_level, d_bf, kmer_sum)
    take_in(0, [0])
    open_filter()
    swap(last_t, keep[0], keep[1], keep[2])
    take_in(2, [0])
    small_step(0)
    take_in(0, rest_of)
    across(0)
    take_in(f_at, [0])
    open_chunk(last_t)
    small_step(1)
    write_out()
    take_in(f_at, rest_of)
    filter_across()
    take_in(2, rest_of)
    across(1)
    for b in range(2, bits):
        small_step(b)
    small_across()
    take_in(2 * last_t, [0])
    take_in(2 * last_t, rest_of)
    across(last_t)
    filter_ring()
    small_back()
    finish_chunk(0)
    finish_chunk(1)
    finish_chunk(last_t)
    sems.arrived(back_base, small_out.at[1 - core], here)
    for mask in range(1, n_dp):
        sems.arrived(ring_base + mask - 1, filt_out.at[flip(dp, mask)], here)
    sems.drain()


def finish_kernel(
    n_taps, layer, mlp_sum, filt, small, embedding, gain_in, taps,
    layer_out_h, grad_emb_h, grad_gain_h, grad_conv_h, filt_out_h, grad_mid_h, mlp_out_h,
    grad_emb, grad_gain, grad_conv, filt_out, grad_mid, sem,
):
    moves = (
        (layer, layer_out_h), (mlp_sum, mlp_out_h), (filt_out, filt_out_h),
        (grad_emb, grad_emb_h), (grad_gain, grad_gain_h), (grad_conv, grad_conv_h), (grad_mid, grad_mid_h),
    )
    copies = [pltpu.make_async_copy(a, b, sem.at[n]) for n, (a, b) in enumerate(moves)]
    copies[0].start()
    copies[1].start()
    n_dp, rows, wide = filt.shape
    lanes_in = filt_out.shape[1] // wide
    for i in range(n_dp):
        top, left = i // lanes_in * rows, i % lanes_in * wide
        filt_out[top : top + rows, left : left + wide] = filt[i].astype(F32)
    copies[2].start()
    channels = embedding.shape[1]
    sums = jnp.concatenate([small[0], small[1]], 0)
    emb = embedding[...]
    gain = gain_in[...].reshape(1, channels)
    base_scale = lax.rsqrt(jnp.mean(emb * emb, axis=1, keepdims=True) + 1e-6)
    unit = emb * base_scale
    base_norm = (unit * gain).astype(BF16).astype(F32)
    d_norm = jnp.zeros(emb.shape, F32)
    for k in range(n_taps):
        part = sums[4 * k : 4 * k + 4, :]
        d_norm = d_norm + part * taps[k : k + 1, :]
        grad_conv[k : k + 1, :] = jnp.sum(part * base_norm, axis=0, keepdims=True)
    grad_gain[...] = jnp.sum(d_norm * unit, axis=0)
    d_unit = d_norm * gain
    base_sum = sums[4 * n_taps : 4 * n_taps + 4, :]
    grad_emb[...] = base_sum + base_scale * (d_unit - unit * jnp.mean(d_unit * unit, axis=1, keepdims=True))
    grad_mid[...] = sums[4 * n_taps + 8 : 4 * n_taps + 9, :].reshape(channels)
    for copy in copies[3:]:
        copy.start()
    for copy in copies:
        copy.wait()


def on_device(tokens, embedding, gain_in, conv_taps, long_filter, gain_mid, mlp_weights, cotangent):
    n_dp, n_seq = lax.axis_size("dp"), lax.axis_size("seq")
    own_rows, block_len = long_filter.shape
    channels = own_rows * n_seq
    local_len = tokens.shape[1]
    lanes_in = n_dp
    while block_len % (lanes_in * 128):
        lanes_in //= 2
    wide = block_len // lanes_in
    table = jnp.asarray(dct_table(block_len).T)
    taps = conv_taps.T
    n_taps = taps.shape[0]
    pairs, bits = n_dp // 2, n_dp.bit_length() - 1
    part = mlp_weights.shape[0] // n_dp
    hidden = mlp_weights.shape[0] // 3
    chunk = part // N_TILES
    upper = color_rows(chunk)
    cols = channels // n_seq
    piece = (own_rows // (n_dp // lanes_in), wide)
    rows_half = (4 * n_taps + 16) // 2
    main = pack_rows(chunk, cols)
    packed = (main, 128) if main else (chunk, cols)
    orders = [[*range(bits - 1)], [*range(1, bits - 1)] + [0] if bits > 1 else []]
    two = 2 * local_len

    def v(shape, dtype=BF16):
        return pltpu.VMEM(shape, dtype)

    stage_bufs = []
    for c in range(2 * N_TILES + 2):
        order = orders[c % 2]
        split = n_seq // 2
        if c < 2 * N_TILES:
            tail = (chunk - upper if c % 2 else upper, channels)
        else:
            tail = (n_seq - split if c % 2 else split,) + piece
        for s in range(bits - 1):
            stage_bufs.append(v((len(stage_masks(order, s, pairs)),) + tail))
    n_sems = sem_count(n_dp, n_seq, lanes_in)
    vmem = pl.BlockSpec(memory_space=pltpu.VMEM)
    hbm = pl.BlockSpec(memory_space=pltpu.HBM)
    cot = cotangent[0]
    operands = [tokens, embedding, gain_in, gain_mid, taps, long_filter, table, mlp_weights, cot]
    operands = [pltpu.with_memory_space_constraint(x, pltpu.HBM) for x in operands]
    layer, mlp_sum, filt, small = pl.pallas_call(
        lambda *refs: mega_kernel(n_dp, n_seq, lanes_in, *refs),
        out_shape=(
            jax.ShapeDtypeStruct(cot.shape, BF16),
            jax.ShapeDtypeStruct((part, cols), F32),
            jax.ShapeDtypeStruct((n_dp,) + piece, BF16),
            jax.ShapeDtypeStruct((2, rows_half, channels), F32),
        ),
        in_specs=[hbm] * 9,
        out_specs=[vmem] * 4,
        scratch_shapes=[
            v(tokens.shape, jnp.int32),
            v(embedding.shape, F32),
            v(gain_in.shape, F32),
            v(gain_mid.shape, F32),
            v(taps.shape, F32),
            v(long_filter.shape, F32),
            v(table.shape),
            v(mlp_weights.shape),
            v(cot.shape),
            v((lanes_in, n_seq, own_rows, wide)),
            v((n_seq,) + tokens.shape, jnp.int32),
            v((channels, block_len), F32),
            v((2, channels, block_len)),
            v((channels, two), F32),
            v((channels, two)),
            v((channels, two), F32),
            v((channels, two), F32),
            v((N_TILES, hidden // N_TILES, two), F32),
        ]
        + [
            v((N_TILES, 2, pairs, chunk, channels)),
            v((N_TILES, pairs, chunk, channels)),
            v((N_TILES, pairs, chunk, channels)),
            v((N_TILES, n_seq) + packed),
            v((N_TILES, n_seq - 1) + packed),
            v((3, hidden // N_TILES, two)),
            v((2, pairs, n_seq) + piece),
            v((pairs, n_seq) + piece),
            v((pairs, n_seq) + piece),
            v((n_seq - 1,) + piece),
            v((2, rows_half, channels), F32),
            v((bits, rows_half, channels), F32),
            v((bits, rows_half, channels), F32),
            v((n_seq, rows_half, channels), F32),
        ]
        + stage_bufs
        + [
            pltpu.SemaphoreType.DMA((9,)),
            pltpu.SemaphoreType.DMA((n_sems,)),
            pltpu.SemaphoreType.DMA((n_sems,)),
        ],
        compiler_params=pltpu.CompilerParams(
            collective_id=0, has_side_effects=True, vmem_limit_bytes=34 * 2**20
        ),
        name="mega",
    )(*operands)
    layer_out, grad_emb, grad_gain, grad_conv, grad_filter, grad_mid, grad_mlp = pl.pallas_call(
        lambda *refs: finish_kernel(n_taps, *refs),
        out_shape=(
            jax.ShapeDtypeStruct(cot.shape, BF16),
            jax.ShapeDtypeStruct(embedding.shape, F32),
            jax.ShapeDtypeStruct(gain_in.shape, F32),
            jax.ShapeDtypeStruct(taps.shape, F32),
            jax.ShapeDtypeStruct(long_filter.shape, F32),
            jax.ShapeDtypeStruct(gain_mid.shape, F32),
            jax.ShapeDtypeStruct((part, cols), F32),
        ),
        in_specs=[vmem] * 7,
        out_specs=[hbm] * 7,
        scratch_shapes=[
            v(embedding.shape, F32),
            v(gain_in.shape, F32),
            v(taps.shape, F32),
            v(long_filter.shape, F32),
            v(gain_mid.shape, F32),
            pltpu.SemaphoreType.DMA((7,)),
        ],
        compiler_params=pltpu.CompilerParams(vmem_limit_bytes=8 * 2**20),
        name="finish",
    )(layer, mlp_sum, filt, small, embedding, gain_in, taps)
    return layer_out[None], grad_emb, grad_gain, grad_conv.T, grad_filter, grad_mid, grad_mlp


def solution(mesh):
    placed = (P("dp", "seq"), P(), P(), P(), P("seq", None), P(), P(), P("dp", None, "seq"))
    return jax.shard_map(
        on_device,
        mesh=mesh,
        in_specs=placed,
        out_specs=(P("dp", None, "seq"), P(), P(), P(), P("seq", None), P(), P("dp", "seq")),
        check_vma=False,
    )
```
